32 devices in a mesh: parts: 2 (over y), tensor: 4 (over z), dp: 2 (over x), pipe: 2 (over core).
Axes of the slice: x: 2, y: 2, z: 4, core: 2. Of those that a mesh axis runs over, the one named last changes fastest.
Arguments:
- queries: bfloat16 [8, 16384], P(('parts', 'dp'), 'tensor'), parts along dimension 0, may hold values from -7 to 7
- key_cache: bfloat16 [8, 8, 4096, 128], P(('parts', 'dp'), None, ('tensor', 'pipe')), parts along dimension 0, may hold values from -7 to 7
- value_cache: bfloat16 [8, 8, 4096, 128], P(('parts', 'dp'), None, ('tensor', 'pipe')), parts along dimension 0, may hold values from -6 to 6
- lengths: int32 [8], P(('parts', 'dp')), parts along dimension 0, may hold values from 2 to 4096, as said below
- languages: int32 [8], P(('parts', 'dp')), parts along dimension 0, may hold values from 0 to 31, as said below
- adapter: bfloat16 [9, 32, 512, 2048], P(None, ('dp', 'pipe'), 'tensor'), may hold values from -1.5 to 1.5
Outputs:
- adapted: bfloat16 [8, 16384], P(('parts', 'dp', 'pipe'), 'tensor'), parts along dimension 0
The draws below stay inside these ranges and needn't reach their ends.
There are 2 independent parts, one for each index of `parts`. The reference program is written for one: setup_inputs(seed, part) draws one part's arguments, and reference() takes and returns one part's arrays. A program takes and returns all parts, laid end to end along the dimension named above; an argument that names none is the same for every part. Nothing has to cross between parts.
Inputs may be any that keep to these rules, and one draw needn't show every extreme that they name: `lengths`: the first row of a part is full. languages fall into 4 groups of 8 consecutive ids; no group is named by more than 2 rows of a part, and one group is named by exactly 2.
All inputs are finite; a program needn't handle non-finite values.
Results may differ from the reference program's by a relative error of at most 0.022.
Values may be sent and summed in bfloat16 or wider, within the bound.
No kernel may reach another device: no remote copies, remote signals or barrier semaphores. Data moves between devices by JAX's collectives and lax.ppermute only.
A program may use at most 192 MiB of HBM per device.

```python
import math
import jax
import jax.numpy as jnp
from jax import lax

HQ = 128
KVH = 8
HD = 128
D = 16384
B = 64
STRETCHES = 512
LEVELS = 9
LANGS = 32
CACHE = 4096
ROWS = 4
HOLDERS = 4
CAPACITY = 2


def draw_queries(key, part):
    own_key = jax.random.fold_in(key, 21)
    shape = (ROWS, KVH, HQ // KVH, HD)
    entries = jax.random.normal(own_key, shape, jnp.float32)
    return entries.reshape(ROWS, HQ * HD).astype(jnp.bfloat16)


def draw_key_cache(key, part):
    own_key = jax.random.fold_in(key, 22)
    shape = (ROWS, KVH, CACHE, HD)
    entries = jax.random.normal(own_key, shape, jnp.float32)
    return entries.astype(jnp.bfloat16)


def draw_value_cache(key, part):
    own_key = jax.random.fold_in(key, 26)
    noise_key, drift_key = jax.random.split(own_key, 2)
    shape = (ROWS, KVH, CACHE, HD)
    position = jnp.arange(CACHE, dtype=jnp.float32)[None, None, :, None] / CACHE
    rough = jnp.clip(0.8 * jax.random.normal(noise_key, shape, jnp.float32), -2.4, 2.4)
    drift = jax.random.uniform(drift_key, (ROWS, KVH, 1, HD), jnp.float32, -1.0, 1.0)
    ramp = 0.25 + 1.75 * position
    return (rough + drift * ramp).astype(jnp.bfloat16)


def draw_lengths(key, part):
    own_key = jax.random.fold_in(key, 23)
    drawn = jax.random.randint(own_key, (ROWS,), 2, CACHE + 1, dtype=jnp.int32)
    return jnp.where(jnp.arange(ROWS) == 0, CACHE, drawn).astype(jnp.int32)


def draw_languages(key, part):
    own_key = jax.random.fold_in(key, 25)
    first_key, pool_key, order_key, within_key = jax.random.split(own_key, 4)
    share_count = LANGS // HOLDERS
    busiest = jax.random.randint(first_key, (), 0, HOLDERS, dtype=jnp.int32)
    others = (busiest + 1 + jnp.arange(HOLDERS - 1, dtype=jnp.int32)) % HOLDERS
    pool = jax.random.permutation(pool_key, jnp.repeat(others, CAPACITY))
    holders = jnp.concatenate([jnp.full((CAPACITY,), busiest, jnp.int32), pool[:ROWS - CAPACITY].astype(jnp.int32)])
    holders = jax.random.permutation(order_key, holders)
    within = jax.random.randint(within_key, (ROWS,), 0, share_count, dtype=jnp.int32)
    return (holders * share_count + within).astype(jnp.int32)


def draw_adapter(key, part):
    own_key = jax.random.fold_in(key, 24)
    shape = (LEVELS, LANGS, STRETCHES, B // 2, B)
    noise = 0.04 * jax.random.normal(own_key, shape, jnp.float32)
    level_ids = jnp.arange(LEVELS)[:, None, None, None, None]
    stretch_ids = jnp.arange(STRETCHES)[None, None, :, None, None]
    side = stretch_ids // 2 ** level_ids % 2
    row_ids = jnp.arange(B // 2)[None, None, None, :, None]
    column_ids = jnp.arange(B)[None, None, None, None, :]
    diagonal = jnp.where(column_ids == side * (B // 2) + row_ids, 1.0, 0.0)
    return (diagonal + noise).reshape(LEVELS, LANGS, STRETCHES, B // 2 * B).astype(jnp.bfloat16)


def setup_inputs(seed: int = 0, part: int = 0) -> dict:
    streams_of = jax.random.split(jax.random.key(seed), 7)
    part_splits = jax.random.split(jax.random.fold_in(streams_of[6], part), 7)
    return {
        "queries": draw_queries(jax.random.fold_in(jax.random.fold_in(streams_of[6], part), 71), part),
        "key_cache": draw_key_cache(jax.random.fold_in(jax.random.fold_in(streams_of[6], part), 71), part),
        "value_cache": draw_value_cache(jax.random.fold_in(jax.random.fold_in(streams_of[6], part), 71), part),
        "lengths": draw_lengths(jax.random.fold_in(jax.random.fold_in(streams_of[6], part), 71), part),
        "languages": draw_languages(jax.random.fold_in(jax.random.fold_in(streams_of[6], part), 71), part),
        "adapter": draw_adapter(jax.random.fold_in(streams_of[6], 71), part),
    }


def attend_row(query_row, key_row, value_row, length):
    group_size = HQ // KVH
    grouped = query_row.reshape(KVH, group_size, HD).astype(jnp.float32)
    scores = jnp.einsum('gjd,gpd->gjp', grouped, key_row.astype(jnp.float32)) / math.sqrt(HD)
    visible = (jnp.arange(CACHE, dtype=jnp.int32) < length)[None, None, :]
    peak_score = lax.optimization_barrier(jnp.max(jnp.where(visible, scores, -1e+30), axis=-1, keepdims=True))
    weights = jnp.where(visible, jnp.exp(scores - peak_score), 0.0)
    totals = lax.optimization_barrier(jnp.sum(weights, axis=-1))
    rounded = lax.optimization_barrier(weights.astype(jnp.bfloat16)).astype(jnp.float32)
    weighted = jnp.einsum('gjp,gpd->gjd', rounded, value_row.astype(jnp.float32))
    return (weighted / totals[..., None]).reshape(HQ * HD).astype(jnp.bfloat16)

def adapt_row(hidden_row, tables):
    half_block = B // 2
    current = hidden_row
    for level_index in range(LEVELS):
        span_e = 2 ** level_index
        groups = STRETCHES // (2 * span_e)
        split = current.reshape(groups, 2, span_e, half_block).astype(jnp.float32)
        paired = jnp.concatenate([split[:, 0], split[:, 1]], axis=-1)
        table = tables[level_index].reshape(groups, 2, span_e, half_block, B).astype(jnp.float32)
        result = jnp.einsum('aeb,asehb->aseh', paired, table).reshape(D)
        current = result.astype(jnp.bfloat16)
    return current

def reference(queries, key_cache, value_cache, lengths, languages, adapter):

    def attend(items):
        return attend_row(items[0], items[1], items[2], items[3])
    attended = lax.map(attend, (queries, key_cache, value_cache, lengths))

    def adapt(items):
        return adapt_row(items[0], lax.dynamic_index_in_dim(adapter, items[1], 1, False))
    return lax.map(adapt, (attended, languages))
```

```python
import functools
import math

import jax
import jax.numpy as jnp
from jax import lax
from jax.experimental import pallas as pl
from jax.experimental.pallas import tpu as pltpu
from jax.sharding import PartitionSpec as P

HQ = 128
KVH = 8
HD = 128
B = 64
HALF = B // 2
LANES = 128
SLOTS = 2
GROUP = HQ // KVH
WIDE = HALF * B
NEG = -1e30

VMEM = pl.BlockSpec(memory_space=pltpu.VMEM)
SMEM = pl.BlockSpec(memory_space=pltpu.SMEM)
ANY = pl.BlockSpec(memory_space=pl.ANY)


def exchange(blocks, axis, count):
    out = [blocks[0]]
    for k in range(1, count):
        route = [(i, i ^ k) for i in range(count)]
        out.append(lax.ppermute(blocks[k], axis, route))
    return out


def iota(shape, dim):
    return lax.broadcasted_iota(jnp.int32, shape, dim)


def attend_kernel(count, idx_ref, len_ref, *refs):
    q_refs, (key_hbm, value_hbm), out_refs = refs[:count], refs[count:count + 2], refs[count + 2:2 * count + 2]
    q_buf, key_buf, value_buf, out_buf, sems = refs[2 * count + 2:]
    rows, share = q_buf.shape[1], q_buf.shape[2]
    span = key_buf.shape[2]
    stages = 2
    per = KVH // stages
    copies = []
    for r in range(rows):
        for h in range(stages):
            part = pl.ds(h * per, per)
            pair = []
            for n, (src, dst) in enumerate(((key_hbm, key_buf), (value_hbm, value_buf))):
                copy = pltpu.make_async_copy(src.at[r, part], dst.at[r, part], sems.at[n, r, h])
                copy.start()
                pair.append(copy)
            copies.append(pair)
    t = idx_ref[0]
    offset = (t * idx_ref[4] + idx_ref[2]) * span
    for k in range(count):
        q_buf[t ^ k] = q_refs[k][...]
    size = min(GROUP, share)
    lane = iota((size, LANES), 1)
    for r in range(rows):
        visible = offset + iota((size, span), 1) < len_ref[r]
        for h in range(stages):
            for copy in copies[r * stages + h]:
                copy.wait()
            for g in range(h * per, (h + 1) * per):
                for part in range(GROUP // size):
                    head = g * GROUP + part * size
                    s, at = head // share, head % share
                    q = q_buf[s, r, at:at + size]
                    scores = lax.dot_general(
                        q, key_buf[r, g], (((1,), (1,)), ((), ())), preferred_element_type=jnp.float32
                    ) * (1.0 / math.sqrt(HD))
                    top = jnp.max(jnp.where(visible, scores, NEG), axis=1, keepdims=True)
                    top = top.astype(jnp.bfloat16).astype(jnp.float32)
                    weights = jnp.where(visible, jnp.exp(scores - top), 0.0)
                    total = jnp.sum(weights, axis=1, keepdims=True)
                    weighted = jnp.dot(
                        weights.astype(jnp.bfloat16), value_buf[r, g], preferred_element_type=jnp.float32
                    )
                    out_buf[s, r, at:at + size, 0:LANES] = weighted.astype(jnp.bfloat16)
                    out_buf[s, r, at:at + size, LANES:] = stats(top, total, lane)
    for k in range(count):
        out_refs[k][...] = out_buf[t ^ k]


def stats(top, total, lane):
    coarse = total.astype(jnp.bfloat16).astype(jnp.float32)
    return jnp.where(lane == 0, top, jnp.where(lane == 1, coarse, total - coarse)).astype(jnp.bfloat16)


def merge(parts):
    tops = [part[:, LANES:LANES + 1] for part in parts]
    peak = functools.reduce(jnp.maximum, tops)
    total, weighted = 0.0, 0.0
    for part, top in zip(parts, tops):
        factor = jnp.exp(top - peak)
        total = total + factor * (part[:, LANES + 1:LANES + 2] + part[:, LANES + 2:LANES + 3])
        weighted = weighted + factor * part[:, :LANES]
    return peak, total, weighted


def attend(idx, lengths, queries, key_cache, value_cache):
    count = len(queries)
    rows, share, _ = queries[0].shape
    span = key_cache.shape[2]
    chunk = jax.ShapeDtypeStruct((rows, share, 2 * LANES), jnp.bfloat16)
    return pl.pallas_call(
        functools.partial(attend_kernel, count),
        out_shape=[chunk] * count,
        in_specs=[SMEM, SMEM] + [VMEM] * count + [ANY, ANY],
        out_specs=[VMEM] * count,
        scratch_shapes=[
            pltpu.VMEM((count, rows, share, HD), jnp.bfloat16),
            pltpu.VMEM((rows, KVH, span, HD), jnp.bfloat16),
            pltpu.VMEM((rows, KVH, span, HD), jnp.bfloat16),
            pltpu.VMEM((count, rows, share, 2 * LANES), jnp.bfloat16),
            pltpu.SemaphoreType.DMA((2, rows, 2)),
        ],
        name="attend",
    )(idx, lengths, *queries, key_cache, value_cache)


def merge_kernel(count, *refs):
    out = refs[count]
    rows, share, _ = out.shape
    lane = iota((share, LANES), 1)
    for r in range(rows):
        peak, total, weighted = merge([refs[k][r].astype(jnp.float32) for k in range(count)])
        out[r, :, 0:LANES] = weighted.astype(jnp.bfloat16)
        out[r, :, LANES:] = stats(peak, total, lane)


def merged(parts):
    return pl.pallas_call(
        functools.partial(merge_kernel, len(parts)),
        out_shape=jax.ShapeDtypeStruct(parts[0].shape, parts[0].dtype),
        in_specs=[VMEM] * len(parts),
        out_specs=VMEM,
        name="merge",
    )(*parts)


def one_hot(cond):
    return jnp.where(cond, 1.0, 0.0).astype(jnp.bfloat16)


def level(own, partner, upper, table, sums):
    lane_upper = iota(own.shape, 1) // HALF % 2
    paired = jnp.where(lane_upper == upper, own, partner).astype(jnp.bfloat16)
    stretch = own.shape[0] // SLOTS
    products = []
    for s in range(SLOTS):
        x = paired[s * stretch:(s + 1) * stretch]
        products.append(
            jnp.concatenate(
                [table[s, :, c * LANES:(c + 1) * LANES] * x for c in range(WIDE // LANES)], axis=1
            )
        )
    y = jnp.dot(jnp.concatenate(products, axis=0), sums, preferred_element_type=jnp.float32)
    return y.astype(jnp.bfloat16).astype(jnp.float32)


def packed(x):
    quarter = x.shape[0] // 4
    block = iota((quarter, LANES), 1) // HALF
    out = x[0:quarter]
    for n in range(1, 4):
        out = jnp.where(block == n, x[n * quarter:(n + 1) * quarter], out)
    return out.astype(jnp.bfloat16)


def unpacked(z):
    row, col = iota((LANES, LANES), 0), iota((LANES, LANES), 1)
    return jnp.concatenate(
        [
            jnp.dot(z, one_hot(row == n * HALF + col % HALF), preferred_element_type=jnp.float32)
            for n in range(4)
        ],
        axis=0,
    )


def slots_of(idx_ref, lang_ref, share):
    d, p, pipe = idx_ref[1], idx_ref[2], idx_ref[4]
    home = d * pipe + p
    near, rows = lang_ref.shape
    found = jnp.int32(0)
    row_ids = [jnp.int32(-1)] * SLOTS
    langs = [jnp.int32(0)] * SLOTS
    for k in range(near):
        for i in range(rows):
            lang = lang_ref[k, i]
            mine = lang // share == home
            for s in range(SLOTS):
                take = mine & (found == s)
                row_ids[s] = jnp.where(take, (d ^ k) * rows + i, row_ids[s])
                langs[s] = jnp.where(take, lang - home * share, langs[s])
            found = found + mine.astype(jnp.int32)
    return row_ids, langs


def local_kernel(count, local, pipe_count, idx_ref, lang_ref, *refs):
    parts, (sums_ref, table_hbm), (x_ref, z_ref, far_ref) = refs[:count], refs[count:count + 2], refs[count + 2:count + 5]
    part_buf, table_buf, sems = refs[count + 5:]
    levels, share = table_hbm.shape[0], table_hbm.shape[1]
    rows = part_buf.shape[1]
    heads = part_buf.shape[2]
    row_ids, langs = slots_of(idx_ref, lang_ref, share)
    copies = []
    for k in range(levels):
        for s in range(SLOTS):
            dst = table_buf.at[k, s] if k < local else far_ref.at[k - local, s]
            copy = pltpu.make_async_copy(table_hbm.at[k, langs[s]], dst, sems.at[k, s])
            copy.start()
            copies.append(copy)
    for k in range(count):
        part_buf[k] = parts[k][...]
    stretch = table_buf.shape[2]
    per_head = HD // HALF
    home = idx_ref[1] * pipe_count + idx_ref[2]
    lift = one_hot(iota((stretch, heads), 0) // per_head == iota((stretch, heads), 1))
    place = iota((stretch, LANES), 1) // HALF == iota((stretch, LANES), 0) % per_head
    spread = one_hot(iota((LANES, LANES), 0) % HALF == iota((LANES, LANES), 1) % HALF)
    current = []
    for s in range(SLOTS):
        row = jnp.maximum(row_ids[s], 0)
        near, i = row // rows, row % rows
        _, total, weighted = merge(
            [
                part_buf[(near * pipe_count + c) ^ home, i].astype(jnp.float32)
                for c in range(pipe_count)
            ]
        )
        attended = (weighted / total).astype(jnp.bfloat16)
        tall = jnp.dot(lift, attended, preferred_element_type=jnp.float32)
        tall = jnp.where(place, tall, 0.0).astype(jnp.bfloat16)
        current.append(jnp.dot(tall, spread, preferred_element_type=jnp.float32))
    x = jnp.concatenate(current, axis=0)
    index = iota(x.shape, 0)
    sums = sums_ref[...]
    for k in range(local):
        reach = 1 << k
        upper = index // reach % 2
        ahead = jnp.roll(x, -reach, axis=0)
        behind = jnp.roll(x, reach, axis=0)
        partner = jnp.where(upper == 0, ahead, behind)
        for s in range(SLOTS):
            copies[k * SLOTS + s].wait()
        x = level(x, partner, upper, table_buf.at[k], sums)
    x_ref[...] = x.astype(jnp.bfloat16)
    z_ref[...] = packed(x)
    for copy in copies[local * SLOTS:]:
        copy.wait()


def local_levels(idx, langs, parts, sums, adapter, local, pipe_count):
    levels, _, stretch, wide = adapter.shape
    count = len(parts)
    shape = (SLOTS * stretch, LANES)
    return pl.pallas_call(
        functools.partial(local_kernel, count, local, pipe_count),
        out_shape=[
            jax.ShapeDtypeStruct(shape, jnp.bfloat16),
            jax.ShapeDtypeStruct((shape[0] // 4, LANES), jnp.bfloat16),
            jax.ShapeDtypeStruct((levels - local, SLOTS, stretch, wide), jnp.bfloat16),
        ],
        in_specs=[SMEM, SMEM] + [VMEM] * (count + 1) + [ANY],
        out_specs=[VMEM] * 3,
        scratch_shapes=[
            pltpu.VMEM((count,) + parts[0].shape, jnp.bfloat16),
            pltpu.VMEM((local, SLOTS, stretch, wide), jnp.bfloat16),
            pltpu.SemaphoreType.DMA((levels, SLOTS)),
        ],
        compiler_params=pltpu.CompilerParams(vmem_limit_bytes=48 << 20),
        name="local_levels",
    )(idx, langs, *parts, sums, adapter)


def far_level(bit, n, idx_ref, x_ref, z_ref, sums_ref, far_ref):
    x = x_ref[...].astype(jnp.float32)
    upper = idx_ref[0] // (1 << bit) % 2
    return level(x, unpacked(z_ref[...]), upper, far_ref.at[n], sums_ref[...])


def cross_kernel(bit, n, idx_ref, x_ref, z_ref, sums_ref, far_ref, x_out, z_out):
    x = far_level(bit, n, idx_ref, x_ref, z_ref, sums_ref, far_ref)
    x_out[...] = x.astype(jnp.bfloat16)
    z_out[...] = packed(x)


def cross_level(idx, x, z, sums, far, bit, n):
    return pl.pallas_call(
        functools.partial(cross_kernel, bit, n),
        out_shape=[
            jax.ShapeDtypeStruct(x.shape, x.dtype),
            jax.ShapeDtypeStruct(z.shape, z.dtype),
        ],
        in_specs=[SMEM] + [VMEM] * 4,
        out_specs=[VMEM] * 2,
        compiler_params=pltpu.CompilerParams(vmem_limit_bytes=32 << 20),
        name="cross_level",
    )(idx, x, z, sums, far)


def last_kernel(bit, n, count, share, pipe_count, idx_ref, lang_ref, x_ref, z_ref, sums_ref, far_ref, *refs):
    outs, done = refs[:count], refs[count]
    row_ids, _ = slots_of(idx_ref, lang_ref, share)
    x = far_level(bit, n, idx_ref, x_ref, z_ref, sums_ref, far_ref)
    stretch = x.shape[0] // SLOTS
    per_head = HD // HALF
    heads = stretch // per_head
    lower = one_hot(iota((heads, stretch), 1) // per_head == iota((heads, stretch), 0))
    place = iota((stretch, LANES), 1) // HALF == iota((stretch, LANES), 0) % per_head
    home = idx_ref[1] * pipe_count + idx_ref[2]
    flat = []
    for s in range(SLOTS):
        tall = jnp.where(place, x[s * stretch:(s + 1) * stretch], 0.0).astype(jnp.bfloat16)
        flat.append(jnp.dot(lower, tall, preferred_element_type=jnp.float32))
    for k in range(count):
        second = (row_ids[1] == (home ^ k)).astype(jnp.float32)
        outs[k][...] = jnp.where(second == 1.0, flat[1], flat[0]).astype(jnp.bfloat16)


def last_level(idx, langs, x, z, sums, far, bit, n, count, share, pipe_count):
    stretch = x.shape[0] // SLOTS
    heads = stretch * HALF // HD
    return pl.pallas_call(
        functools.partial(last_kernel, bit, n, count, share, pipe_count),
        out_shape=[jax.ShapeDtypeStruct((heads, HD), jnp.bfloat16)] * count,
        in_specs=[SMEM, SMEM] + [VMEM] * 4,
        out_specs=[VMEM] * count,
        scratch_shapes=[pltpu.SMEM((1,), jnp.int32)],
        compiler_params=pltpu.CompilerParams(vmem_limit_bytes=32 << 20),
        name="last_level",
    )(idx, langs, x, z, sums, far)


def shards(queries, key_cache, value_cache, lengths, languages, adapter):
    tensor, near, pipe = (lax.axis_size(a) for a in ("tensor", "dp", "pipe"))
    rows = queries.shape[0]
    share = HQ // tensor
    holders = near * pipe
    levels, lang_share, stretch, _ = adapter.shape
    local = stretch.bit_length() - 1
    t, d, p = (lax.axis_index(a) for a in ("tensor", "dp", "pipe"))
    idx = jnp.stack([t, d, p, jnp.int32(near), jnp.int32(pipe)]).astype(jnp.int32)

    own = queries.reshape(rows, share, HD)
    spread = exchange([own] * tensor, "tensor", tensor)
    langs = jnp.stack(exchange([languages] * near, "dp", near))
    parts = attend(idx, lengths, spread, key_cache, value_cache)
    parts = exchange(parts, "tensor", tensor)
    part = merged(parts)
    parts = exchange([part] * holders, ("dp", "pipe"), holders)
    shape = (WIDE, LANES)
    sums = one_hot(iota(shape, 0) // B == iota(shape, 1) % HALF)
    x, z, far = local_levels(idx, langs, parts, sums, adapter, local, pipe)
    for n in range(levels - local):
        z = lax.ppermute(z, "tensor", [(i, i ^ (1 << n)) for i in range(tensor)])
        if n < levels - local - 1:
            x, z = cross_level(idx, x, z, sums, far, n, n)
        else:
            outs = last_level(idx, langs, x, z, sums, far, n, n, holders, lang_share, pipe)
    outs = exchange(outs, ("dp", "pipe"), holders)
    own_lang = jnp.where(p == 0, languages[0], languages[1])
    source = (own_lang // lang_share) ^ (d * pipe + p)
    result = outs[0]
    for k in range(1, holders):
        result = jnp.where(source == k, outs[k], result)
    return result.reshape(1, share * HD)


def solution(mesh):
    in_specs = (
        P(("parts", "dp"), "tensor"),
        P(("parts", "dp"), None, ("tensor", "pipe"), None),
        P(("parts", "dp"), None, ("tensor", "pipe"), None),
        P(("parts", "dp")),
        P(("parts", "dp")),
        P(None, ("dp", "pipe"), "tensor", None),
    )
    out_specs = P(("parts", "dp", "pipe"), "tensor")
    return jax.shard_map(shards, mesh=mesh, in_specs=in_specs, out_specs=out_specs, check_vma=False)
```

```python
import functools
import math

import jax
import jax.numpy as jnp
from jax import lax
from jax.experimental import pallas as pl
from jax.experimental.pallas import tpu as pltpu
from jax.sharding import PartitionSpec as P

HQ = 128
KVH = 8
HD = 128
B = 64
HALF = B // 2
LANES = 128
SLOTS = 2
GROUP = HQ // KVH
WIDE = HALF * B
NEG = -1e30
EARLY = 4
STATS = 16

VMEM = pl.BlockSpec(memory_space=pltpu.VMEM)
SMEM = pl.BlockSpec(memory_space=pltpu.SMEM)
HBM = pl.BlockSpec(memory_space=pltpu.HBM)
ANY = pl.BlockSpec(memory_space=pl.ANY)


def exchange(blocks, axis, count):
    out = [blocks[0]]
    for k in range(1, count):
        route = [(i, i ^ k) for i in range(count)]
        out.append(lax.ppermute(blocks[k], axis, route))
    return out


def iota(shape, dim):
    return lax.broadcasted_iota(jnp.int32, shape, dim)


def load_kernel(key_hbm, value_hbm, key_ref, value_ref, sums_ref, sems):
    rows = key_hbm.shape[0]
    half = KVH // 2
    copies = []
    for r in range(rows):
        for h in range(2):
            part = pl.ds(h * half, half)
            for n, (src, dst) in enumerate(((key_hbm, key_ref), (value_hbm, value_ref))):
                copy = pltpu.make_async_copy(src.at[r, part], dst.at[r, part], sems.at[n, r, h])
                copy.start()
                copies.append(copy)
    sums_ref[...] = one_hot(iota(sums_ref.shape, 0) // B == iota(sums_ref.shape, 1) % HALF)
    for copy in copies:
        copy.wait()


def load(key_cache, value_cache):
    cache = jax.ShapeDtypeStruct(key_cache.shape, key_cache.dtype)
    return pl.pallas_call(
        load_kernel,
        out_shape=[cache, cache, jax.ShapeDtypeStruct((WIDE, LANES), jnp.bfloat16)],
        in_specs=[HBM, HBM],
        out_specs=[VMEM] * 3,
        scratch_shapes=[pltpu.SemaphoreType.DMA((2, key_cache.shape[0], 2))],
        compiler_params=pltpu.CompilerParams(vmem_limit_bytes=8 << 20),
        name="load",
    )(key_cache, value_cache)


def slots_of(lang_ref, share):
    home = holder()
    d = lax.axis_index("dp")
    near, rows = lang_ref.shape
    found = jnp.int32(0)
    row_ids = [jnp.int32(-1)] * SLOTS
    langs = [jnp.int32(0)] * SLOTS
    for k in range(near):
        for i in range(rows):
            lang = lang_ref[k, i]
            mine = lang // share == home
            for s in range(SLOTS):
                take = mine & (found == s)
                row_ids[s] = jnp.where(take, (d ^ k) * rows + i, row_ids[s])
                langs[s] = jnp.where(take, lang - home * share, langs[s])
            found = found + mine.astype(jnp.int32)
    return row_ids, langs


def holder():
    return lax.axis_index(("dp", "pipe"))


def start_tables(first, langs, table_hbm, table_ref, sems):
    copies = []
    for k in range(table_ref.shape[0]):
        for s in range(SLOTS):
            copy = pltpu.make_async_copy(table_hbm.at[first + k, langs[s]], table_ref.at[k, s], sems.at[k, s])
            copy.start()
            copies.append(copy)
    return copies


def attend_kernel(count, lang_any, len_ref, *refs):
    q_refs, (key_ref, value_ref, table_hbm) = refs[:count], refs[count:count + 3]
    out_refs, (table_ref, slot_ref) = refs[count + 3:2 * count + 3], refs[2 * count + 3:2 * count + 5]
    score_buf, lang_ref, lang_sem, sems = refs[2 * count + 5:]
    lang_copy = pltpu.make_async_copy(lang_any, lang_ref, lang_sem)
    lang_copy.start()
    rows = q_refs[0].shape[0]
    share = q_refs[0].shape[1] // HD
    span = key_ref.shape[2]
    t = lax.axis_index("tensor")
    offset = lax.axis_index(("tensor", "pipe")) * span
    size = min(GROUP, share)
    tall = size * rows
    chunks = [(k, c) for k in range(count) for c in range(share // size)]

    def pick(parts):
        which = iota(parts[0].shape, 0) % rows
        out = parts[0]
        for r in range(1, rows):
            out = jnp.where(which == r, parts[r], out)
        return out

    for n, (k, c) in enumerate(chunks):
        group = ((t ^ k) * share + c * size) // GROUP
        q = jnp.concatenate(
            [q_refs[k][:, h * HD:(h + 1) * HD] for h in range(c * size, (c + 1) * size)], axis=0
        )
        score_buf[n] = pick(
            [
                lax.dot_general(
                    q, key_ref[r, group], (((1,), (1,)), ((), ())), preferred_element_type=jnp.float32
                )
                for r in range(rows)
            ]
        ) * (1.0 / math.sqrt(HD))

    lang_copy.wait()
    row_ids, langs = slots_of(lang_ref, table_hbm.shape[1])
    copies = start_tables(0, langs, table_hbm, table_ref, sems)
    row = iota(slot_ref.shape, 0)
    own = lang_ref[0, lax.axis_index("pipe")] // table_hbm.shape[1]
    slots = jnp.where(row == SLOTS, own ^ holder(), -1)
    for s in range(SLOTS):
        slots = jnp.where(row == s, row_ids[s], slots)
    slot_ref[...] = slots

    block = share * rows
    spot = iota((tall, LANES), 1) % block - iota((tall, LANES), 0)
    tops, totals = [0.0] * count, [0.0] * count
    visible = offset + iota((tall, span), 1) < len_ref[...][:, 0:1]
    for n, (k, c) in enumerate(chunks):
        group = ((t ^ k) * share + c * size) // GROUP
        scores = score_buf[n]
        top = jnp.max(jnp.where(visible, scores, NEG), axis=1, keepdims=True)
        top = top.astype(jnp.bfloat16).astype(jnp.float32)
        weights = jnp.where(visible, jnp.exp(scores - top), 0.0)
        total = jnp.sum(weights, axis=1, keepdims=True)
        weights = weights.astype(jnp.bfloat16)
        weighted = pick(
            [
                jnp.dot(weights, value_ref[r, group], preferred_element_type=jnp.float32)
                for r in range(rows)
            ]
        )
        out_refs[k][c * tall:(c + 1) * tall] = weighted.astype(jnp.bfloat16)
        here = spot == c * tall
        tops[k] = tops[k] + jnp.sum(jnp.where(here, top, 0.0), axis=0, keepdims=True)
        totals[k] = totals[k] + jnp.sum(jnp.where(here, total, 0.0), axis=0, keepdims=True)
    for k in range(count):
        out_refs[k][block:] = stats(tops[k], totals[k])
    for copy in copies:
        copy.wait()


def stats(top, total):
    coarse = total.astype(jnp.bfloat16).astype(jnp.float32)
    row = iota((STATS, LANES), 0)
    out = jnp.where(row == 0, top, jnp.where(row == 1, coarse, jnp.where(row == 2, total - coarse, 0.0)))
    return out.astype(jnp.bfloat16)


def factors(parts):
    tops, totals = [], []
    for part in parts:
        rows = part[part.shape[0] - STATS:].astype(jnp.float32)
        tops.append(rows[0:1])
        totals.append(rows[1:2] + rows[2:3])
    peak = functools.reduce(jnp.maximum, tops)
    scale = [jnp.exp(top - peak) for top in tops]
    return scale, peak, sum(f * total for f, total in zip(scale, totals))


def weigh(scale, mask, block):
    coarse = scale.astype(jnp.bfloat16).astype(jnp.float32)
    side = iota((1, LANES), 1) // block
    both = jnp.where(side == 0, coarse, jnp.where(side == 1, scale - coarse, 0.0))
    return jnp.where(mask, both, 0.0).astype(jnp.bfloat16)


def stacked(parts, block):
    return jnp.concatenate([part[:block] for part in parts for _ in range(LANES // block)], axis=0)


def attend(langs, lengths, queries, key_cache, value_cache, adapter, early):
    count = len(queries)
    rows, width = queries[0].shape
    share = width // HD
    _, _, stretch, wide = adapter.shape
    size = min(GROUP, share)
    span = key_cache.shape[2]
    chunk = jax.ShapeDtypeStruct((share * rows + STATS, LANES), jnp.bfloat16)
    lengths = jnp.broadcast_to(jnp.tile(lengths, size)[:, None], (size * rows, LANES))
    return pl.pallas_call(
        functools.partial(attend_kernel, count),
        out_shape=[chunk] * count + [
            jax.ShapeDtypeStruct((early, SLOTS, stretch, wide), jnp.bfloat16),
            jax.ShapeDtypeStruct((8, LANES), jnp.int32),
        ],
        in_specs=[ANY] + [VMEM] * (count + 3) + [HBM],
        out_specs=[VMEM] * (count + 2),
        scratch_shapes=[
            pltpu.VMEM((count * share // size, size * rows, span), jnp.float32),
            pltpu.SMEM(langs.shape, jnp.int32),
            pltpu.SemaphoreType.DMA,
            pltpu.SemaphoreType.DMA((early, SLOTS)),
        ],
        compiler_params=pltpu.CompilerParams(vmem_limit_bytes=24 << 20),
        name="attend",
    )(langs, lengths, *queries, key_cache, value_cache, adapter)


def fetch_kernel(first, lang_ref, after_ref, table_hbm, table_ref, sems):
    _, langs = slots_of(lang_ref, table_hbm.shape[1])
    for copy in start_tables(first, langs, table_hbm, table_ref, sems):
        copy.wait()


def fetch(langs, after, adapter, first):
    levels, _, stretch, wide = adapter.shape
    return pl.pallas_call(
        functools.partial(fetch_kernel, first),
        out_shape=jax.ShapeDtypeStruct((levels - first, SLOTS, stretch, wide), jnp.bfloat16),
        in_specs=[SMEM, ANY, HBM],
        out_specs=VMEM,
        scratch_shapes=[pltpu.SemaphoreType.DMA((levels - first, SLOTS))],
        compiler_params=pltpu.CompilerParams(vmem_limit_bytes=16 << 20),
        name="fetch",
    )(langs, after, adapter)


def merge_kernel(count, *refs):
    out = refs[count]
    parts = [refs[k][...] for k in range(count)]
    block = out.shape[0] - STATS
    scale, peak, total = factors(parts)
    mask = iota((block, LANES), 1) % block == iota((block, LANES), 0)
    matrix = jnp.concatenate([weigh(f, mask, block) for f in scale], axis=1)
    weighted = jnp.dot(matrix, stacked(parts, block), preferred_element_type=jnp.float32)
    out[:block] = weighted.astype(jnp.bfloat16)
    out[block:] = stats(peak, total)


def merged(parts):
    return pl.pallas_call(
        functools.partial(merge_kernel, len(parts)),
        out_shape=jax.ShapeDtypeStruct(parts[0].shape, parts[0].dtype),
        in_specs=[VMEM] * len(parts),
        out_specs=VMEM,
        compiler_params=pltpu.CompilerParams(vmem_limit_bytes=8 << 20),
        name="merge",
    )(*parts)


def one_hot(cond):
    return jnp.where(cond, 1.0, 0.0).astype(jnp.bfloat16)


def level(own, partner, upper, table, sums):
    lane_upper = iota(own.shape, 1) // HALF % 2
    paired = jnp.where(lane_upper == upper, own, partner).astype(jnp.bfloat16)
    stretch = own.shape[0] // SLOTS
    products = []
    for s in range(SLOTS):
        x = paired[s * stretch:(s + 1) * stretch]
        products.append(
            jnp.concatenate(
                [table[s, :, c * LANES:(c + 1) * LANES] * x for c in range(WIDE // LANES)], axis=1
            )
        )
    y = jnp.dot(jnp.concatenate(products, axis=0), sums, preferred_element_type=jnp.float32)
    return y.astype(jnp.bfloat16).astype(jnp.float32)


def packed(x):
    quarter = x.shape[0] // 4
    block = iota((quarter, LANES), 1) // HALF
    out = x[0:quarter]
    for n in range(1, 4):
        out = jnp.where(block == n, x[n * quarter:(n + 1) * quarter], out)
    return out.astype(jnp.bfloat16)


def unpacked(z):
    row, col = iota((LANES, LANES), 0), iota((LANES, LANES), 1)
    return jnp.concatenate(
        [
            jnp.dot(z, one_hot(row == n * HALF + col % HALF), preferred_element_type=jnp.float32)
            for n in range(4)
        ],
        axis=0,
    )


def local_kernel(count, local, rows, pipe_count, slot_ref, sums_ref, near_ref, late_ref, *refs):
    parts, (x_ref, z_ref) = refs[:count], refs[count:]
    early, _, stretch, _ = near_ref.shape
    near = count // pipe_count
    block = parts[0].shape[0] - STATS
    per_head = HD // HALF
    d = lax.axis_index("dp")
    parts = [part[...] for part in parts]
    shape = (stretch, LANES)
    lane = iota(shape, 1) % block
    same_head = iota(shape, 0) // per_head == lane // rows
    place = iota(shape, 1) // HALF == iota(shape, 0) % per_head
    spread = one_hot(iota((LANES, LANES), 0) % HALF == iota((LANES, LANES), 1) % HALF)
    columns = [[] for _ in range(SLOTS)]
    for k in range(near):
        pair = parts[k * pipe_count:(k + 1) * pipe_count]
        scale, _, total = factors(pair)
        row = (d ^ k) * rows + lane % rows
        for s in range(SLOTS):
            mask = same_head & (row == slot_ref[s:s + 1])
            columns[s] += [weigh(f / total, mask, block) for f in scale]
    matrix = jnp.concatenate([jnp.concatenate(c, axis=1) for c in columns], axis=0)
    tall = jnp.dot(matrix, stacked(parts, block), preferred_element_type=jnp.float32)
    place = jnp.concatenate([place] * SLOTS, axis=0)
    tall = jnp.where(place, tall, 0.0).astype(jnp.bfloat16)
    x = jnp.dot(tall, spread, preferred_element_type=jnp.float32)
    index = iota(x.shape, 0)
    sums = sums_ref[...]
    for k in range(local):
        reach = 1 << k
        upper = index // reach % 2
        ahead = jnp.roll(x, -reach, axis=0)
        behind = jnp.roll(x, reach, axis=0)
        partner = jnp.where(upper == 0, ahead, behind)
        x = level(x, partner, upper, near_ref.at[k] if k < early else late_ref.at[k - early], sums)
    x_ref[...] = x.astype(jnp.bfloat16)
    z_ref[...] = packed(x)


def local_levels(slots, parts, sums, tables, late, local, rows, pipe_count):
    stretch = tables.shape[2]
    count = len(parts)
    shape = (SLOTS * stretch, LANES)
    return pl.pallas_call(
        functools.partial(local_kernel, count, local, rows, pipe_count),
        out_shape=[
            jax.ShapeDtypeStruct(shape, jnp.bfloat16),
            jax.ShapeDtypeStruct((shape[0] // 4, LANES), jnp.bfloat16),
        ],
        in_specs=[VMEM] * (count + 4),
        out_specs=[VMEM] * 2,
        compiler_params=pltpu.CompilerParams(vmem_limit_bytes=24 << 20),
        name="local_levels",
    )(slots, sums, tables, late, *parts)


def far_level(bit, n, x_ref, z_ref, sums_ref, far_ref):
    x = x_ref[...].astype(jnp.float32)
    upper = lax.axis_index("tensor") // (1 << bit) % 2
    return level(x, unpacked(z_ref[...]), upper, far_ref.at[n], sums_ref[...])


def cross_kernel(bit, n, x_ref, z_ref, sums_ref, far_ref, x_out, z_out):
    x = far_level(bit, n, x_ref, z_ref, sums_ref, far_ref)
    x_out[...] = x.astype(jnp.bfloat16)
    z_out[...] = packed(x)


def cross_level(x, z, sums, far, bit, n):
    return pl.pallas_call(
        functools.partial(cross_kernel, bit, n),
        out_shape=[
            jax.ShapeDtypeStruct(x.shape, x.dtype),
            jax.ShapeDtypeStruct(z.shape, z.dtype),
        ],
        in_specs=[VMEM] * 4,
        out_specs=[VMEM] * 2,
        compiler_params=pltpu.CompilerParams(vmem_limit_bytes=32 << 20),
        name="cross_level",
    )(x, z, sums, far)


def last_kernel(bit, n, count, slot_ref, x_ref, z_ref, sums_ref, far_ref, *outs):
    x = far_level(bit, n, x_ref, z_ref, sums_ref, far_ref)
    stretch = x.shape[0] // SLOTS
    per_head = HD // HALF
    heads = stretch // per_head
    lower = one_hot(iota((heads, stretch), 1) // per_head == iota((heads, stretch), 0))
    place = iota((stretch, LANES), 1) // HALF == iota((stretch, LANES), 0) % per_head
    home = holder()
    flat = []
    for s in range(SLOTS):
        tall = jnp.where(place, x[s * stretch:(s + 1) * stretch], 0.0).astype(jnp.bfloat16)
        flat.append(jnp.dot(lower, tall, preferred_element_type=jnp.float32))
    for k in range(count):
        second = slot_ref[1:2] == (home ^ k)
        outs[k][...] = jnp.where(second, flat[1], flat[0]).astype(jnp.bfloat16)


def last_level(slots, x, z, sums, far, bit, n, count):
    stretch = x.shape[0] // SLOTS
    heads = stretch * HALF // HD
    return pl.pallas_call(
        functools.partial(last_kernel, bit, n, count),
        out_shape=[jax.ShapeDtypeStruct((heads, HD), jnp.bfloat16)] * count,
        in_specs=[VMEM] * 5,
        out_specs=[VMEM] * count,
        compiler_params=pltpu.CompilerParams(vmem_limit_bytes=32 << 20),
        name="last_level",
    )(slots, x, z, sums, far)


def pick_kernel(count, slot_ref, *refs):
    parts, out = refs[:count], refs[count]
    which = slot_ref[SLOTS:SLOTS + 1]
    row = parts[0][...].astype(jnp.float32)
    for k in range(1, count):
        row = jnp.where(which == k, parts[k][...].astype(jnp.float32), row)
    row = row.astype(jnp.bfloat16)
    for h in range(row.shape[0]):
        out[0:1, h * HD:(h + 1) * HD] = row[h:h + 1]


def picked(slots, parts):
    heads = parts[0].shape[0]
    count = len(parts)
    return pl.pallas_call(
        functools.partial(pick_kernel, count),
        out_shape=jax.ShapeDtypeStruct((1, heads * HD), jnp.bfloat16),
        in_specs=[VMEM] * (count + 1),
        out_specs=VMEM,
        compiler_params=pltpu.CompilerParams(vmem_limit_bytes=8 << 20),
        name="pick",
    )(slots, *parts)


def shards(queries, key_cache, value_cache, lengths, languages, adapter):
    tensor, near, pipe = (lax.axis_size(a) for a in ("tensor", "dp", "pipe"))
    rows = queries.shape[0]
    holders = near * pipe
    levels, _, stretch, _ = adapter.shape
    local = stretch.bit_length() - 1
    langs = jnp.stack(exchange([languages] * near, "dp", near))
    spread = exchange([queries] * tensor, "tensor", tensor)
    keys, values, sums = load(
        pltpu.with_memory_space_constraint(key_cache, pltpu.HBM),
        pltpu.with_memory_space_constraint(value_cache, pltpu.HBM),
    )
    early = min(EARLY, local)
    *parts, tables, slots = attend(langs, lengths, spread, keys, values, adapter, early)
    late = fetch(langs, parts[0], adapter, early)
    parts = exchange(parts, "tensor", tensor)
    part = merged(parts)
    parts = exchange([part] * holders, ("dp", "pipe"), holders)
    x, z = local_levels(slots, parts, sums, tables, late, local, rows, pipe)
    for n in range(levels - local):
        z = lax.ppermute(z, "tensor", [(i, i ^ (1 << n)) for i in range(tensor)])
        at = local + n - early
        if n < levels - local - 1:
            x, z = cross_level(x, z, sums, late, n, at)
        else:
            outs = last_level(slots, x, z, sums, late, n, at, holders)
    outs = exchange(outs, ("dp", "pipe"), holders)
    return picked(slots, outs)


def solution(mesh):
    in_specs = (
        P(("parts", "dp"), "tensor"),
        P(("parts", "dp"), None, ("tensor", "pipe"), None),
        P(("parts", "dp"), None, ("tensor", "pipe"), None),
        P(("parts", "dp")),
        P(("parts", "dp")),
        P(None, ("dp", "pipe"), "tensor", None),
    )
    out_specs = P(("parts", "dp", "pipe"), "tensor")
    return jax.shard_map(shards, mesh=mesh, in_specs=in_specs, out_specs=out_specs, check_vma=False)
```

```python
import functools
import math

import jax
import jax.numpy as jnp
from jax import lax
from jax.experimental import pallas as pl
from jax.experimental.pallas import tpu as pltpu
from jax.sharding import PartitionSpec as P

HQ = 128
KVH = 8
HD = 128
B = 64
HALF = B // 2
LANES = 128
SLOTS = 2
GROUP = HQ // KVH
WIDE = HALF * B
NEG = -1e30
FLOOR = -1e29
FIRST = 3
STATS = 16

VMEM = pl.BlockSpec(memory_space=pltpu.VMEM)
SMEM = pl.BlockSpec(memory_space=pltpu.SMEM)
HBM = pl.BlockSpec(memory_space=pltpu.HBM)
ANY = pl.BlockSpec(memory_space=pl.ANY)


def exchange(blocks, axis, count):
    out = [blocks[0]]
    for k in range(1, count):
        route = [(i, i ^ k) for i in range(count)]
        out.append(lax.ppermute(blocks[k], axis, route))
    return out


def by_parity(tensor):
    return HQ // tensor >= GROUP


def half_of(index, tensor):
    if by_parity(tensor):
        half = index
        for n in range(1, (tensor - 1).bit_length()):
            half = half ^ (index >> n)
        return half & 1
    return index // (tensor // 2)


def reach_of(i, p, tensor):
    if by_parity(tensor):
        return (i << 1) | (half_of(i, tensor) ^ p)
    return p * (tensor // 2) + i


def place_of(shard, tensor):
    return shard >> 1 if by_parity(tensor) else shard % (tensor // 2)


def cores_exchange(blocks, tensor):
    out = []
    for i, block in enumerate(blocks):
        route = [(2 * t + p, 2 * (t ^ reach_of(i, p, tensor)) + p) for t in range(tensor) for p in range(2)]
        out.append(lax.ppermute(block, ("tensor", "pipe"), route))
    return out


def iota(shape, dim):
    return lax.broadcasted_iota(jnp.int32, shape, dim)


def start_half(flip, src_hbm, dst_ref, sems):
    rows = dst_ref.shape[0]
    tensor = lax.axis_size("tensor")
    half = half_of(lax.axis_index("tensor"), tensor) ^ lax.axis_index("pipe") ^ flip
    size = HQ // tensor // GROUP if by_parity(tensor) else KVH // 2
    copies = []
    for r in range(rows):
        for j in range(KVH // 2 // size):
            src = pl.ds(reach_of(j, half, tensor) * size if by_parity(tensor) else half * size, size)
            copy = pltpu.make_async_copy(src_hbm.at[r, src], dst_ref.at[r, pl.ds(j * size, size)], sems.at[r, j])
            copy.start()
            copies.append(copy)
    return copies


def send_kernel(*refs):
    caches, outs, sems = refs[:2], refs[2:4], refs[4]
    copies = []
    for n in range(2):
        copies += start_half(1, caches[n], outs[n], sems.at[n])
    for copy in copies:
        copy.wait()


def send_halves(key_cache, value_cache):
    rows, _, span, _ = key_cache.shape
    half = jax.ShapeDtypeStruct((rows, KVH // 2, span, HD), key_cache.dtype)
    return pl.pallas_call(
        send_kernel,
        out_shape=[half, half],
        in_specs=[HBM, HBM],
        out_specs=[VMEM, VMEM],
        scratch_shapes=[pltpu.SemaphoreType.DMA((2, rows, KVH // 2))],
        compiler_params=pltpu.CompilerParams(vmem_limit_bytes=8 << 20),
        name="send_halves",
    )(key_cache, value_cache)


def slots_of(lang_refs, rows, share):
    home = holder()
    d = lax.axis_index("dp")
    found = jnp.int32(0)
    row_ids = [jnp.int32(-1)] * SLOTS
    langs = [jnp.int32(0)] * SLOTS
    for k, lang_ref in enumerate(lang_refs):
        for i in range(rows):
            lang = lang_ref[i]
            mine = lang // share == home
            for s in range(SLOTS):
                take = mine & (found == s)
                row_ids[s] = jnp.where(take, (d ^ k) * rows + i, row_ids[s])
                langs[s] = jnp.where(take, lang - home * share, langs[s])
            found = found + mine.astype(jnp.int32)
    return row_ids, langs


def holder():
    return lax.axis_index(("dp", "pipe"))


def start_tables(first, langs, table_hbm, table_ref, sems):
    copies = []
    for k in range(table_ref.shape[0]):
        for s in range(SLOTS):
            copy = pltpu.make_async_copy(table_hbm.at[first + k, langs[s]], table_ref.at[k, s], sems.at[k, s])
            copy.start()
            copies.append(copy)
    return copies


def own_kernel(count, *refs):
    q_refs, (key_hbm, value_hbm) = refs[:count], refs[count:count + 2]
    wide_ref, score_ref, value_ref, sums_ref, key_buf, sems = refs[count + 2:]
    key_copies = start_half(0, key_hbm, key_buf, sems.at[0])
    value_copies = start_half(0, value_hbm, value_ref, sems.at[1])
    rows = q_refs[0].shape[0]
    chunks, tall, _ = wide_ref.shape
    size = tall // rows
    sums_ref[...] = one_hot(iota(sums_ref.shape, 0) // B == iota(sums_ref.shape, 1) % HALF)
    which = iota((tall, HD), 0) % rows
    wide = []
    for n in range(chunks):
        k, c = divmod(n, chunks // count)
        q = jnp.concatenate(
            [q_refs[k][:, h * HD:(h + 1) * HD] for h in range(c * size, (c + 1) * size)], axis=0
        )
        q = jnp.concatenate([jnp.where(which == r, q, jnp.zeros_like(q)) for r in range(rows)], axis=1)
        wide_ref[n] = q
        wide.append(q)
    for copy in key_copies:
        copy.wait()
    for n in range(chunks):
        score_ref[n] = scores_of(wide[n], key_buf, group_of(n, chunks, count, size))
    for copy in value_copies:
        copy.wait()


def beside(ref, group):
    return jnp.concatenate([ref[r, group] for r in range(ref.shape[0])], axis=1)


def scores_of(wide, key_ref, group):
    return lax.dot_general(
        wide, beside(key_ref, group), (((1,), (1,)), ((), ())), preferred_element_type=jnp.float32
    )


def group_of(n, chunks, count, size):
    k, c = divmod(n, chunks // count)
    tensor = 2 * count
    shard = lax.axis_index("tensor") ^ reach_of(k, lax.axis_index("pipe"), tensor)
    return (place_of(shard, tensor) * (HQ // tensor) + c * size) // GROUP


def attend_own(queries, key_cache, value_cache):
    count = len(queries)
    rows, width = queries[0].shape
    share = width // HD
    size = min(GROUP, share)
    span = key_cache.shape[2]
    chunks, tall = count * share // size, size * rows
    half = (rows, KVH // 2, span, HD)
    return pl.pallas_call(
        functools.partial(own_kernel, count),
        out_shape=[
            jax.ShapeDtypeStruct((chunks, tall, rows * HD), jnp.bfloat16),
            jax.ShapeDtypeStruct((chunks, tall, span), jnp.float32),
            jax.ShapeDtypeStruct(half, jnp.bfloat16),
            jax.ShapeDtypeStruct((WIDE, LANES), jnp.bfloat16),
        ],
        in_specs=[VMEM] * count + [HBM] * 2,
        out_specs=[VMEM] * 4,
        scratch_shapes=[
            pltpu.VMEM(half, jnp.bfloat16),
            pltpu.SemaphoreType.DMA((2, rows, KVH // 2)),
        ],
        compiler_params=pltpu.CompilerParams(vmem_limit_bytes=16 << 20),
        cost_estimate=pl.CostEstimate(flops=int(2e10), bytes_accessed=1 << 22, transcendentals=0),
        name="attend_own",
    )(*queries, key_cache, value_cache)


def attend_kernel(count, near, lang_share, *refs):
    scalars, refs = refs[:near + 1], refs[near + 1:]
    wide_ref, score_ref, own_value_ref, key_ref, value_ref = refs[:5]
    out_refs, (slot_ref, lang_ref, lang_sems) = refs[5:count + 5], refs[count + 5:]
    lang_copies = [
        pltpu.make_async_copy(src, lang_ref.at[k], lang_sems.at[k]) for k, src in enumerate(scalars)
    ]
    for copy in lang_copies:
        copy.start()
    rows, _, span, _ = key_ref.shape
    chunks, tall, _ = wide_ref.shape
    size = tall // rows
    share = size * (chunks // count)
    t, p = lax.axis_index("tensor"), lax.axis_index("pipe")
    other = [
        scores_of(wide_ref[n], key_ref, group_of(n, chunks, count, size)) for n in range(chunks)
    ]
    for copy in lang_copies:
        copy.wait()
    row_ids, langs = slots_of([lang_ref.at[k] for k in range(near)], rows, lang_share)
    row = iota(slot_ref.shape, 0)
    own = lang_ref[0, p] // lang_share
    slots = jnp.where(row == SLOTS, own ^ holder(), -1)
    for s in range(SLOTS):
        slots = jnp.where(row == s, row_ids[s], slots)
        slots = jnp.where(row == SLOTS + 1 + s, langs[s], slots)
    slot_ref[...] = slots

    block = share * rows
    spot = iota((tall, LANES), 1) % block - iota((tall, LANES), 0)
    tops, totals = [0.0] * count, [0.0] * count
    place = iota((tall, 2 * span), 1)
    start = jnp.where(place < span, p, (1 ^ p) - 1) + 2 * t
    which = iota((tall, 2 * span), 0) % rows
    length = lang_ref[near, 0]
    for r in range(1, rows):
        length = jnp.where(which == r, lang_ref[near, r], length)
    visible = start * span + place < length
    for n in range(chunks):
        k, c = divmod(n, chunks // count)
        group = group_of(n, chunks, count, size)
        scores = jnp.concatenate([score_ref[n], other[n]], axis=1)
        scores = jnp.where(visible, scores * (1.0 / math.sqrt(HD)), NEG)
        top = jnp.maximum(jnp.max(scores, axis=1, keepdims=True), FLOOR)
        top = top.astype(jnp.bfloat16).astype(jnp.float32)
        weights = jnp.exp(scores - top)
        total = jnp.sum(weights, axis=1, keepdims=True)
        weights = weights.astype(jnp.bfloat16)
        both = sum(
            jnp.dot(
                weights[:, side * span:(side + 1) * span],
                beside(values, group),
                preferred_element_type=jnp.float32,
            )
            for side, values in enumerate((own_value_ref, value_ref))
        )
        which = iota((tall, LANES), 0) % rows
        weighted = both[:, :HD]
        for r in range(1, rows):
            weighted = jnp.where(which == r, both[:, r * HD:(r + 1) * HD], weighted)
        out_refs[k][c * tall:(c + 1) * tall] = weighted.astype(jnp.bfloat16)
        here = spot == c * tall
        tops[k] = tops[k] + jnp.sum(jnp.where(here, top, 0.0), axis=0, keepdims=True)
        totals[k] = totals[k] + jnp.sum(jnp.where(here, total, 0.0), axis=0, keepdims=True)
    for k in range(count):
        out_refs[k][block:] = stats(tops[k], totals[k])


def stats(top, total):
    coarse = total.astype(jnp.bfloat16).astype(jnp.float32)
    row = iota((STATS, LANES), 0)
    out = jnp.where(row == 0, top, jnp.where(row == 1, coarse, jnp.where(row == 2, total - coarse, 0.0)))
    return out.astype(jnp.bfloat16)


def factors(parts):
    tops, totals = [], []
    for part in parts:
        rows = part[part.shape[0] - STATS:].astype(jnp.float32)
        tops.append(rows[0:1])
        totals.append(rows[1:2] + rows[2:3])
    peak = functools.reduce(jnp.maximum, tops)
    scale = [jnp.exp(top - peak) for top in tops]
    return scale, peak, sum(f * total for f, total in zip(scale, totals))


def weigh(scale, mask, block):
    coarse = scale.astype(jnp.bfloat16).astype(jnp.float32)
    side = iota((1, LANES), 1) // block
    both = jnp.where(side == 0, coarse, jnp.where(side == 1, scale - coarse, 0.0))
    return jnp.where(mask, both, 0.0).astype(jnp.bfloat16)


def stacked(parts, block):
    return jnp.concatenate([part[:block] for part in parts for _ in range(LANES // block)], axis=0)


def attend(langs, lengths, wide, scores, own_value, key, value, count, lang_share):
    near = len(langs)
    chunks, tall, _ = wide.shape
    rows = key.shape[0]
    chunk = jax.ShapeDtypeStruct((chunks // count * tall + STATS, LANES), jnp.bfloat16)
    return pl.pallas_call(
        functools.partial(attend_kernel, count, near, lang_share),
        out_shape=[chunk] * count + [jax.ShapeDtypeStruct((8, LANES), jnp.int32)],
        in_specs=[ANY] * (near + 1) + [VMEM] * 5,
        out_specs=[VMEM] * (count + 1),
        scratch_shapes=[
            pltpu.SMEM((near + 1, rows), jnp.int32),
            pltpu.SemaphoreType.DMA((near + 1,)),
        ],
        compiler_params=pltpu.CompilerParams(vmem_limit_bytes=16 << 20),
        name="attend",
    )(*langs, lengths, wide, scores, own_value, key, value)


def fetch_kernel(first, slot_ref, _, table_hbm, table_ref, sems):
    places = slot_ref[SLOTS + 1:2 * SLOTS + 1].astype(jnp.float32)
    langs = [jnp.max(places[s:s + 1]).astype(jnp.int32) for s in range(SLOTS)]
    for copy in start_tables(first, langs, table_hbm, table_ref, sems):
        copy.wait()


def fetch(slots, after, adapter, first, count):
    _, _, stretch, wide = adapter.shape
    return pl.pallas_call(
        functools.partial(fetch_kernel, first),
        out_shape=jax.ShapeDtypeStruct((count, SLOTS, stretch, wide), jnp.bfloat16),
        in_specs=[VMEM, ANY, HBM],
        out_specs=VMEM,
        scratch_shapes=[pltpu.SemaphoreType.DMA((count, SLOTS))],
        compiler_params=pltpu.CompilerParams(vmem_limit_bytes=16 << 20),
        name="fetch",
    )(slots, after, adapter)


def merge_kernel(count, *refs):
    out = refs[-1]
    parts = [refs[k][...] for k in range(count)]
    block = out.shape[0] - STATS
    scale, peak, total = factors(parts)
    mask = iota((block, LANES), 1) % block == iota((block, LANES), 0)
    matrix = jnp.concatenate([weigh(f, mask, block) for f in scale], axis=1)
    weighted = jnp.dot(matrix, stacked(parts, block), preferred_element_type=jnp.float32)
    out[:block] = weighted.astype(jnp.bfloat16)
    out[block:] = stats(peak, total)


def merged(parts, after):
    return pl.pallas_call(
        functools.partial(merge_kernel, len(parts)),
        out_shape=jax.ShapeDtypeStruct(parts[0].shape, parts[0].dtype),
        in_specs=[VMEM] * len(parts) + [ANY],
        out_specs=VMEM,
        compiler_params=pltpu.CompilerParams(vmem_limit_bytes=8 << 20),
        name="merge",
    )(*parts, after)


def one_hot(cond):
    return jnp.where(cond, 1.0, 0.0).astype(jnp.bfloat16)


def level(own, partner, upper, table, sums):
    lane_upper = iota(own.shape, 1) // HALF % 2
    paired = jnp.where(lane_upper == upper, own, partner).astype(jnp.bfloat16)
    products = jnp.concatenate(
        [table[:, c * LANES:(c + 1) * LANES] * paired for c in range(WIDE // LANES)], axis=1
    )
    y = jnp.dot(products, sums, preferred_element_type=jnp.float32)
    return y.astype(jnp.bfloat16).astype(jnp.float32)


def packed(x):
    quarter = x.shape[0] // 4
    block = iota((quarter, LANES), 1) // HALF
    out = x[0:quarter]
    for n in range(1, 4):
        out = jnp.where(block == n, x[n * quarter:(n + 1) * quarter], out)
    return out.astype(jnp.bfloat16)


def unpacked(z):
    row, col = iota((LANES, LANES), 0), iota((LANES, LANES), 1)
    return jnp.concatenate(
        [
            jnp.dot(z, one_hot(row == n * HALF + col % HALF), preferred_element_type=jnp.float32)
            for n in range(4)
        ],
        axis=0,
    )


def local_kernel(count, groups, local, rows, pipe_count, slot_ref, sums_ref, *refs):
    tables, parts, (x_ref, z_ref) = refs[:groups], refs[groups:groups + count], refs[groups + count:]
    stretch = tables[0].shape[2]
    near = count // pipe_count
    block = parts[0].shape[0] - STATS
    per_head = HD // HALF
    d = lax.axis_index("dp")
    parts = [part[...] for part in parts]
    shape = (stretch, LANES)
    lane = iota(shape, 1) % block
    same_head = iota(shape, 0) // per_head == lane // rows
    place = iota(shape, 1) // HALF == iota(shape, 0) % per_head
    spread = one_hot(iota((LANES, LANES), 0) % HALF == iota((LANES, LANES), 1) % HALF)
    columns = [[] for _ in range(SLOTS)]
    for k in range(near):
        pair = parts[k * pipe_count:(k + 1) * pipe_count]
        scale, _, total = factors(pair)
        row = (d ^ k) * rows + lane % rows
        for s in range(SLOTS):
            mask = same_head & (row == slot_ref[s:s + 1])
            columns[s] += [weigh(f / total, mask, block) for f in scale]
    matrix = jnp.concatenate([jnp.concatenate(c, axis=1) for c in columns], axis=0)
    tall = jnp.dot(matrix, stacked(parts, block), preferred_element_type=jnp.float32)
    place = jnp.concatenate([place] * SLOTS, axis=0)
    tall = jnp.where(place, tall, 0.0).astype(jnp.bfloat16)
    xs = [
        jnp.dot(tall[s * stretch:(s + 1) * stretch], spread, preferred_element_type=jnp.float32)
        for s in range(SLOTS)
    ]
    index = iota(shape, 0)
    sums = sums_ref[...]
    for k in range(local):
        reach = 1 << k
        upper = index // reach % 2
        table, at = table_of(tables, k)
        for s in range(SLOTS):
            ahead = jnp.roll(xs[s], -reach, axis=0)
            behind = jnp.roll(xs[s], reach, axis=0)
            partner = jnp.where(upper == 0, ahead, behind)
            xs[s] = level(xs[s], partner, upper, table.at[at, s], sums)
    x = jnp.concatenate(xs, axis=0)
    x_ref[...] = x.astype(jnp.bfloat16)
    z_ref[...] = packed(x)


def table_of(tables, k):
    for table in tables:
        if k < table.shape[0]:
            return table, k
        k -= table.shape[0]


def local_levels(slots, parts, sums, tables, local, rows, pipe_count):
    stretch = tables[0].shape[2]
    count = len(parts)
    shape = (SLOTS * stretch, LANES)
    return pl.pallas_call(
        functools.partial(local_kernel, count, len(tables), local, rows, pipe_count),
        out_shape=[
            jax.ShapeDtypeStruct(shape, jnp.bfloat16),
            jax.ShapeDtypeStruct((shape[0] // 4, LANES), jnp.bfloat16),
        ],
        in_specs=[VMEM] * (count + len(tables) + 2),
        out_specs=[VMEM] * 2,
        compiler_params=pltpu.CompilerParams(vmem_limit_bytes=24 << 20),
        name="local_levels",
    )(slots, sums, *tables, *parts)


def far_level(bit, n, x_ref, z_ref, sums_ref, far_ref):
    upper = lax.axis_index("tensor") // (1 << bit) % 2
    partner = unpacked(z_ref[...])
    stretch = x_ref.shape[0] // SLOTS
    sums = sums_ref[...]
    out = []
    for s in range(SLOTS):
        part = slice(s * stretch, (s + 1) * stretch)
        out.append(level(x_ref[part].astype(jnp.float32), partner[part], upper, far_ref.at[n, s], sums))
    return jnp.concatenate(out, axis=0)


def cross_kernel(bit, n, x_ref, z_ref, sums_ref, far_ref, x_out, z_out):
    x = far_level(bit, n, x_ref, z_ref, sums_ref, far_ref)
    x_out[...] = x.astype(jnp.bfloat16)
    z_out[...] = packed(x)


def cross_level(x, z, sums, far, bit, n):
    return pl.pallas_call(
        functools.partial(cross_kernel, bit, n),
        out_shape=[
            jax.ShapeDtypeStruct(x.shape, x.dtype),
            jax.ShapeDtypeStruct(z.shape, z.dtype),
        ],
        in_specs=[VMEM] * 4,
        out_specs=[VMEM] * 2,
        compiler_params=pltpu.CompilerParams(vmem_limit_bytes=32 << 20),
        name="cross_level",
    )(x, z, sums, far)


def last_kernel(bit, n, count, slot_ref, x_ref, z_ref, sums_ref, far_ref, *outs):
    x = far_level(bit, n, x_ref, z_ref, sums_ref, far_ref)
    stretch = x.shape[0] // SLOTS
    per_head = HD // HALF
    heads = stretch // per_head
    lower = one_hot(iota((heads, stretch), 1) // per_head == iota((heads, stretch), 0))
    place = iota((stretch, LANES), 1) // HALF == iota((stretch, LANES), 0) % per_head
    home = holder()
    flat = []
    for s in range(SLOTS):
        tall = jnp.where(place, x[s * stretch:(s + 1) * stretch], 0.0).astype(jnp.bfloat16)
        flat.append(jnp.dot(lower, tall, preferred_element_type=jnp.float32))
    for k in range(count):
        second = slot_ref[1:2] == (home ^ k)
        outs[k][...] = jnp.where(second, flat[1], flat[0]).astype(jnp.bfloat16)


def last_level(slots, x, z, sums, far, bit, n, count):
    stretch = x.shape[0] // SLOTS
    heads = stretch * HALF // HD
    return pl.pallas_call(
        functools.partial(last_kernel, bit, n, count),
        out_shape=[jax.ShapeDtypeStruct((heads, HD), jnp.bfloat16)] * count,
        in_specs=[VMEM] * 5,
        out_specs=[VMEM] * count,
        compiler_params=pltpu.CompilerParams(vmem_limit_bytes=32 << 20),
        name="last_level",
    )(slots, x, z, sums, far)


def pick_kernel(count, slot_ref, *refs):
    parts, out = refs[:count], refs[count]
    which = slot_ref[SLOTS:SLOTS + 1]
    row = parts[0][...].astype(jnp.float32)
    for k in range(1, count):
        row = jnp.where(which == k, parts[k][...].astype(jnp.float32), row)
    row = row.astype(jnp.bfloat16)
    for h in range(row.shape[0]):
        out[0:1, h * HD:(h + 1) * HD] = row[h:h + 1]


def picked(slots, parts):
    heads = parts[0].shape[0]
    count = len(parts)
    return pl.pallas_call(
        functools.partial(pick_kernel, count),
        out_shape=jax.ShapeDtypeStruct((1, heads * HD), jnp.bfloat16),
        in_specs=[VMEM] * (count + 1),
        out_specs=VMEM,
        compiler_params=pltpu.CompilerParams(vmem_limit_bytes=8 << 20),
        name="pick",
    )(slots, *parts)


def shards(queries, key_cache, value_cache, lengths, languages, adapter):
    tensor, near, pipe = (lax.axis_size(a) for a in ("tensor", "dp", "pipe"))
    rows = queries.shape[0]
    holders = near * pipe
    levels, lang_share, stretch, _ = adapter.shape
    local = stretch.bit_length() - 1
    caches = [pltpu.with_memory_space_constraint(c, pltpu.HBM) for c in (key_cache, value_cache)]
    swap = [(0, 1), (1, 0)]
    sent = send_halves(*caches)
    other = [lax.ppermute(half, "pipe", swap) for half in sent]
    later, _ = lax.optimization_barrier((languages, sent[0]))
    langs = exchange([later] * near, "dp", near)
    spread = cores_exchange([queries] * (tensor // 2), tensor)
    wide, scores, own_value, sums = attend_own(spread, *caches)
    *parts, slots = attend(
        langs, lengths, wide, scores, own_value, *other, tensor // 2, lang_share
    )
    first = fetch(slots, parts[0], adapter, 0, FIRST)
    part = merged(cores_exchange(parts, tensor), first)
    second = fetch(slots, part, adapter, FIRST, local - FIRST)
    parts = exchange([part] * holders, ("dp", "pipe"), holders)
    x, z = local_levels(slots, parts, sums, (first, second), local, rows, pipe)
    far = fetch(slots, z, adapter, local, levels - local)
    for n in range(levels - local):
        z = lax.ppermute(z, "tensor", [(i, i ^ (1 << n)) for i in range(tensor)])
        if n < levels - local - 1:
            x, z = cross_level(x, z, sums, far, n, n)
        else:
            outs = last_level(slots, x, z, sums, far, n, n, holders)
    outs = exchange(outs, ("dp", "pipe"), holders)
    return picked(slots, outs)


def solution(mesh):
    in_specs = (
        P(("parts", "dp"), "tensor"),
        P(("parts", "dp"), None, ("tensor", "pipe"), None),
        P(("parts", "dp"), None, ("tensor", "pipe"), None),
        P(("parts", "dp")),
        P(("parts", "dp")),
        P(None, ("dp", "pipe"), "tensor", None),
    )
    out_specs = P(("parts", "dp", "pipe"), "tensor")
    return jax.shard_map(shards, mesh=mesh, in_specs=in_specs, out_specs=out_specs, check_vma=False)
```

```python
import functools
import math

import jax
import jax.numpy as jnp
from jax import lax
from jax.experimental import pallas as pl
from jax.experimental.pallas import tpu as pltpu
from jax.sharding import PartitionSpec as P

HQ = 128
KVH = 8
HD = 128
B = 64
HALF = B // 2
LANES = 128
SLOTS = 2
GROUP = HQ // KVH
WIDE = HALF * B
NEG = -1e30
FLOOR = -1e29
FIRST = 2
STATS = 16

VMEM = pl.BlockSpec(memory_space=pltpu.VMEM)
SMEM = pl.BlockSpec(memory_space=pltpu.SMEM)
HBM = pl.BlockSpec(memory_space=pltpu.HBM)
ANY = pl.BlockSpec(memory_space=pl.ANY)


def exchange(blocks, axis, count):
    out = [blocks[0]]
    for k in range(1, count):
        route = [(i, i ^ k) for i in range(count)]
        out.append(lax.ppermute(blocks[k], axis, route))
    return out


def by_parity(tensor):
    return HQ // tensor >= GROUP


def half_of(index, tensor):
    if by_parity(tensor):
        half = index
        for n in range(1, (tensor - 1).bit_length()):
            half = half ^ (index >> n)
        return half & 1
    return index // (tensor // 2)


def reach_of(i, p, tensor):
    if by_parity(tensor):
        return (i << 1) | (half_of(i, tensor) ^ p)
    return p * (tensor // 2) + i


def place_of(shard, tensor):
    return shard >> 1 if by_parity(tensor) else shard % (tensor // 2)


def cores_exchange(blocks, tensor):
    out = []
    for i, block in enumerate(blocks):
        route = [(2 * t + p, 2 * (t ^ reach_of(i, p, tensor)) + p) for t in range(tensor) for p in range(2)]
        out.append(lax.ppermute(block, ("tensor", "pipe"), route))
    return out


def iota(shape, dim):
    return lax.broadcasted_iota(jnp.int32, shape, dim)


def start_half(flip, src_hbm, dst_ref, sems):
    rows = dst_ref.shape[0]
    tensor = lax.axis_size("tensor")
    half = half_of(lax.axis_index("tensor"), tensor) ^ lax.axis_index("pipe") ^ flip
    size = HQ // tensor // GROUP if by_parity(tensor) else KVH // 2
    copies = []
    for r in range(rows):
        for j in range(KVH // 2 // size):
            src = pl.ds(reach_of(j, half, tensor) * size if by_parity(tensor) else half * size, size)
            copy = pltpu.make_async_copy(src_hbm.at[r, src], dst_ref.at[r, pl.ds(j * size, size)], sems.at[r, j])
            copy.start()
            copies.append(copy)
    return copies


def send_kernel(*refs):
    caches, outs, sems = refs[:2], refs[2:4], refs[4]
    copies = []
    for n in range(2):
        copies += start_half(1, caches[n], outs[n], sems.at[n])
    for copy in copies:
        copy.wait()


def send_halves(key_cache, value_cache):
    rows, _, span, _ = key_cache.shape
    half = jax.ShapeDtypeStruct((rows, KVH // 2, span, HD), key_cache.dtype)
    return pl.pallas_call(
        send_kernel,
        out_shape=[half, half],
        in_specs=[HBM, HBM],
        out_specs=[VMEM, VMEM],
        scratch_shapes=[pltpu.SemaphoreType.DMA((2, rows, KVH // 2))],
        compiler_params=pltpu.CompilerParams(vmem_limit_bytes=8 << 20),
        name="send_halves",
    )(key_cache, value_cache)


def slots_of(lang_refs, rows, share):
    home = holder()
    d = lax.axis_index("dp")
    found = jnp.int32(0)
    row_ids = [jnp.int32(-1)] * SLOTS
    langs = [jnp.int32(0)] * SLOTS
    for k, lang_ref in enumerate(lang_refs):
        for i in range(rows):
            lang = lang_ref[i]
            mine = lang // share == home
            for s in range(SLOTS):
                take = mine & (found == s)
                row_ids[s] = jnp.where(take, (d ^ k) * rows + i, row_ids[s])
                langs[s] = jnp.where(take, lang - home * share, langs[s])
            found = found + mine.astype(jnp.int32)
    return row_ids, langs


def holder():
    return lax.axis_index(("dp", "pipe"))


def start_tables(first, langs, table_hbm, table_ref, sems):
    copies = []
    for k in range(table_ref.shape[0]):
        for s in range(SLOTS):
            copy = pltpu.make_async_copy(table_hbm.at[first + k, langs[s]], table_ref.at[k, s], sems.at[k, s])
            copy.start()
            copies.append(copy)
    return copies


def own_kernel(count, *refs):
    q_refs, key_ref = refs[:count], refs[count]
    wide_ref, score_ref, sums_ref = refs[count + 1:]
    rows = q_refs[0].shape[0]
    chunks, tall, _ = wide_ref.shape
    size = tall // rows
    sums_ref[...] = one_hot(iota(sums_ref.shape, 0) // B == iota(sums_ref.shape, 1) % HALF)
    which = iota((tall, HD), 0) % rows
    for n in range(chunks):
        k, c = divmod(n, chunks // count)
        q = jnp.concatenate(
            [q_refs[k][:, h * HD:(h + 1) * HD] for h in range(c * size, (c + 1) * size)], axis=0
        )
        q = jnp.concatenate([jnp.where(which == r, q, jnp.zeros_like(q)) for r in range(rows)], axis=1)
        wide_ref[n] = q
        score_ref[n] = scores_of(q, key_ref, group_of(n, chunks, count, size, True))


def beside(ref, group):
    return jnp.concatenate([ref[r, group] for r in range(ref.shape[0])], axis=1)


def scores_of(wide, key_ref, group):
    return lax.dot_general(
        wide, beside(key_ref, group), (((1,), (1,)), ((), ())), preferred_element_type=jnp.float32
    )


def group_of(n, chunks, count, size, of_all=False):
    k, c = divmod(n, chunks // count)
    tensor = 2 * count
    shard = lax.axis_index("tensor") ^ reach_of(k, lax.axis_index("pipe"), tensor)
    place = shard if of_all else place_of(shard, tensor)
    return (place * (HQ // tensor) + c * size) // GROUP


def attend_own(queries, key_cache):
    count = len(queries)
    rows, width = queries[0].shape
    share = width // HD
    size = min(GROUP, share)
    span = key_cache.shape[2]
    chunks, tall = count * share // size, size * rows
    return pl.pallas_call(
        functools.partial(own_kernel, count),
        out_shape=[
            jax.ShapeDtypeStruct((chunks, tall, rows * HD), jnp.bfloat16),
            jax.ShapeDtypeStruct((chunks, tall, span), jnp.float32),
            jax.ShapeDtypeStruct((WIDE, LANES), jnp.bfloat16),
        ],
        in_specs=[VMEM] * (count + 1),
        out_specs=[VMEM] * 3,
        compiler_params=pltpu.CompilerParams(vmem_limit_bytes=16 << 20),
        name="attend_own",
    )(*queries, key_cache)


def attend_kernel(count, near, lang_share, *refs):
    scalars, refs = refs[:near + 1], refs[near + 1:]
    wide_ref, score_ref, own_value_ref, key_ref, value_ref = refs[:5]
    out_refs, (slot_ref, lang_ref, lang_sems) = refs[5:count + 5], refs[count + 5:]
    lang_copies = [
        pltpu.make_async_copy(src, lang_ref.at[k], lang_sems.at[k]) for k, src in enumerate(scalars)
    ]
    for copy in lang_copies:
        copy.start()
    rows, _, span, _ = key_ref.shape
    chunks, tall, _ = wide_ref.shape
    size = tall // rows
    share = size * (chunks // count)
    t, p = lax.axis_index("tensor"), lax.axis_index("pipe")
    other = [
        scores_of(wide_ref[n], key_ref, group_of(n, chunks, count, size)) for n in range(chunks)
    ]
    for copy in lang_copies:
        copy.wait()
    row_ids, langs = slots_of([lang_ref.at[k] for k in range(near)], rows, lang_share)
    row = iota(slot_ref.shape, 0)
    own = lang_ref[0, p] // lang_share
    slots = jnp.where(row == SLOTS, own ^ holder(), -1)
    for s in range(SLOTS):
        slots = jnp.where(row == s, row_ids[s], slots)
        slots = jnp.where(row == SLOTS + 1 + s, langs[s], slots)
    slot_ref[...] = slots

    block = share * rows
    spot = iota((tall, LANES), 1) % block - iota((tall, LANES), 0)
    tops, totals = [0.0] * count, [0.0] * count
    place = iota((tall, 2 * span), 1)
    start = jnp.where(place < span, p, (1 ^ p) - 1) + 2 * t
    which = iota((tall, 2 * span), 0) % rows
    length = lang_ref[near, 0]
    for r in range(1, rows):
        length = jnp.where(which == r, lang_ref[near, r], length)
    visible = start * span + place < length
    for n in range(chunks):
        k, c = divmod(n, chunks // count)
        group, whole = group_of(n, chunks, count, size), group_of(n, chunks, count, size, True)
        scores = jnp.concatenate([score_ref[n], other[n]], axis=1)
        scores = jnp.where(visible, scores * (1.0 / math.sqrt(HD)), NEG)
        top = jnp.maximum(jnp.max(scores, axis=1, keepdims=True), FLOOR)
        top = top.astype(jnp.bfloat16).astype(jnp.float32)
        weights = jnp.exp(scores - top)
        total = jnp.sum(weights, axis=1, keepdims=True)
        weights = weights.astype(jnp.bfloat16)
        both = sum(
            jnp.dot(
                weights[:, side * span:(side + 1) * span],
                beside(values, place),
                preferred_element_type=jnp.float32,
            )
            for side, (values, place) in enumerate(((own_value_ref, whole), (value_ref, group)))
        )
        which = iota((tall, LANES), 0) % rows
        weighted = both[:, :HD]
        for r in range(1, rows):
            weighted = jnp.where(which == r, both[:, r * HD:(r + 1) * HD], weighted)
        out_refs[k][c * tall:(c + 1) * tall] = weighted.astype(jnp.bfloat16)
        here = spot == c * tall
        tops[k] = tops[k] + jnp.sum(jnp.where(here, top, 0.0), axis=0, keepdims=True)
        totals[k] = totals[k] + jnp.sum(jnp.where(here, total, 0.0), axis=0, keepdims=True)
    for k in range(count):
        out_refs[k][block:] = stats(tops[k], totals[k])


def stats(top, total):
    coarse = total.astype(jnp.bfloat16).astype(jnp.float32)
    row = iota((STATS, LANES), 0)
    out = jnp.where(row == 0, top, jnp.where(row == 1, coarse, jnp.where(row == 2, total - coarse, 0.0)))
    return out.astype(jnp.bfloat16)


def factors(parts):
    tops, totals = [], []
    for part in parts:
        rows = part[part.shape[0] - STATS:].astype(jnp.float32)
        tops.append(rows[0:1])
        totals.append(rows[1:2] + rows[2:3])
    peak = functools.reduce(jnp.maximum, tops)
    scale = [jnp.exp(top - peak) for top in tops]
    return scale, peak, sum(f * total for f, total in zip(scale, totals))


def weigh(scale, mask, block):
    coarse = scale.astype(jnp.bfloat16).astype(jnp.float32)
    side = iota((1, LANES), 1) // block
    both = jnp.where(side == 0, coarse, jnp.where(side == 1, scale - coarse, 0.0))
    return jnp.where(mask, both, 0.0).astype(jnp.bfloat16)


def stacked(parts, block):
    return jnp.concatenate([part[:block] for part in parts for _ in range(LANES // block)], axis=0)


def attend(langs, lengths, wide, scores, own_value, key, value, count, lang_share):
    near = len(langs)
    chunks, tall, _ = wide.shape
    rows = key.shape[0]
    chunk = jax.ShapeDtypeStruct((chunks // count * tall + STATS, LANES), jnp.bfloat16)
    return pl.pallas_call(
        functools.partial(attend_kernel, count, near, lang_share),
        out_shape=[chunk] * count + [jax.ShapeDtypeStruct((8, LANES), jnp.int32)],
        in_specs=[ANY] * (near + 1) + [VMEM] * 5,
        out_specs=[VMEM] * (count + 1),
        scratch_shapes=[
            pltpu.SMEM((near + 1, rows), jnp.int32),
            pltpu.SemaphoreType.DMA((near + 1,)),
        ],
        compiler_params=pltpu.CompilerParams(vmem_limit_bytes=16 << 20),
        name="attend",
    )(*langs, lengths, wide, scores, own_value, key, value)


def fetch_kernel(first, slot_ref, _, table_hbm, table_ref, sems):
    places = slot_ref[SLOTS + 1:2 * SLOTS + 1].astype(jnp.float32)
    langs = [jnp.max(places[s:s + 1]).astype(jnp.int32) for s in range(SLOTS)]
    for copy in start_tables(first, langs, table_hbm, table_ref, sems):
        copy.wait()


def fetch(slots, after, adapter, first, count):
    _, _, stretch, wide = adapter.shape
    return pl.pallas_call(
        functools.partial(fetch_kernel, first),
        out_shape=jax.ShapeDtypeStruct((count, SLOTS, stretch, wide), jnp.bfloat16),
        in_specs=[VMEM, ANY, HBM],
        out_specs=VMEM,
        scratch_shapes=[pltpu.SemaphoreType.DMA((count, SLOTS))],
        compiler_params=pltpu.CompilerParams(vmem_limit_bytes=16 << 20),
        name="fetch",
    )(slots, after, adapter)


def merge_kernel(count, *refs):
    out = refs[-1]
    parts = [refs[k][...] for k in range(count)]
    block = out.shape[0] - STATS
    scale, peak, total = factors(parts)
    mask = iota((block, LANES), 1) % block == iota((block, LANES), 0)
    matrix = jnp.concatenate([weigh(f, mask, block) for f in scale], axis=1)
    weighted = jnp.dot(matrix, stacked(parts, block), preferred_element_type=jnp.float32)
    out[:block] = weighted.astype(jnp.bfloat16)
    out[block:] = stats(peak, total)


def merged(parts, after):
    return pl.pallas_call(
        functools.partial(merge_kernel, len(parts)),
        out_shape=jax.ShapeDtypeStruct(parts[0].shape, parts[0].dtype),
        in_specs=[VMEM] * len(parts) + [ANY],
        out_specs=VMEM,
        compiler_params=pltpu.CompilerParams(vmem_limit_bytes=8 << 20),
        name="merge",
    )(*parts, after)


def one_hot(cond):
    return jnp.where(cond, 1.0, 0.0).astype(jnp.bfloat16)


def level(own, partner, upper, table, sums):
    lane_upper = iota(own.shape, 1) // HALF % 2
    paired = jnp.where(lane_upper == upper, own, partner).astype(jnp.bfloat16)
    products = jnp.concatenate(
        [table[:, c * LANES:(c + 1) * LANES] * paired for c in range(WIDE // LANES)], axis=1
    )
    y = jnp.dot(products, sums, preferred_element_type=jnp.float32)
    return y.astype(jnp.bfloat16).astype(jnp.float32)


def packed(x):
    quarter = x.shape[0] // 4
    block = iota((quarter, LANES), 1) // HALF
    out = x[0:quarter]
    for n in range(1, 4):
        out = jnp.where(block == n, x[n * quarter:(n + 1) * quarter], out)
    return out.astype(jnp.bfloat16)


def unpacked(z):
    row, col = iota((LANES, LANES), 0), iota((LANES, LANES), 1)
    return jnp.concatenate(
        [
            jnp.dot(z, one_hot(row == n * HALF + col % HALF), preferred_element_type=jnp.float32)
            for n in range(4)
        ],
        axis=0,
    )


def local_kernel(count, groups, local, rows, pipe_count, slot_ref, sums_ref, *refs):
    tables, parts, (x_ref, z_ref) = refs[:groups], refs[groups:groups + count], refs[groups + count:]
    stretch = tables[0].shape[2]
    near = count // pipe_count
    block = parts[0].shape[0] - STATS
    per_head = HD // HALF
    d = lax.axis_index("dp")
    parts = [part[...] for part in parts]
    shape = (stretch, LANES)
    lane = iota(shape, 1) % block
    same_head = iota(shape, 0) // per_head == lane // rows
    place = iota(shape, 1) // HALF == iota(shape, 0) % per_head
    spread = one_hot(iota((LANES, LANES), 0) % HALF == iota((LANES, LANES), 1) % HALF)
    columns = [[] for _ in range(SLOTS)]
    for k in range(near):
        pair = parts[k * pipe_count:(k + 1) * pipe_count]
        scale, _, total = factors(pair)
        row = (d ^ k) * rows + lane % rows
        for s in range(SLOTS):
            mask = same_head & (row == slot_ref[s:s + 1])
            columns[s] += [weigh(f / total, mask, block) for f in scale]
    matrix = jnp.concatenate([jnp.concatenate(c, axis=1) for c in columns], axis=0)
    tall = jnp.dot(matrix, stacked(parts, block), preferred_element_type=jnp.float32)
    place = jnp.concatenate([place] * SLOTS, axis=0)
    tall = jnp.where(place, tall, 0.0).astype(jnp.bfloat16)
    xs = [
        jnp.dot(tall[s * stretch:(s + 1) * stretch], spread, preferred_element_type=jnp.float32)
        for s in range(SLOTS)
    ]
    index = iota(shape, 0)
    sums = sums_ref[...]
    for k in range(local):
        reach = 1 << k
        upper = index // reach % 2
        table, at = table_of(tables, k)
        for s in range(SLOTS):
            ahead = jnp.roll(xs[s], -reach, axis=0)
            behind = jnp.roll(xs[s], reach, axis=0)
            partner = jnp.where(upper == 0, ahead, behind)
            xs[s] = level(xs[s], partner, upper, table.at[at, s], sums)
    x = jnp.concatenate(xs, axis=0)
    x_ref[...] = x.astype(jnp.bfloat16)
    z_ref[...] = packed(x)


def table_of(tables, k):
    for table in tables:
        if k < table.shape[0]:
            return table, k
        k -= table.shape[0]


def local_levels(slots, parts, sums, tables, local, rows, pipe_count):
    stretch = tables[0].shape[2]
    count = len(parts)
    shape = (SLOTS * stretch, LANES)
    return pl.pallas_call(
        functools.partial(local_kernel, count, len(tables), local, rows, pipe_count),
        out_shape=[
            jax.ShapeDtypeStruct(shape, jnp.bfloat16),
            jax.ShapeDtypeStruct((shape[0] // 4, LANES), jnp.bfloat16),
        ],
        in_specs=[VMEM] * (count + len(tables) + 2),
        out_specs=[VMEM] * 2,
        compiler_params=pltpu.CompilerParams(vmem_limit_bytes=24 << 20),
        name="local_levels",
    )(slots, sums, *tables, *parts)


def far_level(bit, n, x_ref, z_ref, sums_ref, far_ref):
    upper = lax.axis_index("tensor") // (1 << bit) % 2
    partner = unpacked(z_ref[...])
    stretch = x_ref.shape[0] // SLOTS
    sums = sums_ref[...]
    out = []
    for s in range(SLOTS):
        part = slice(s * stretch, (s + 1) * stretch)
        out.append(level(x_ref[part].astype(jnp.float32), partner[part], upper, far_ref.at[n, s], sums))
    return jnp.concatenate(out, axis=0)


def cross_kernel(bit, n, x_ref, z_ref, sums_ref, far_ref, x_out, z_out):
    x = far_level(bit, n, x_ref, z_ref, sums_ref, far_ref)
    x_out[...] = x.astype(jnp.bfloat16)
    z_out[...] = packed(x)


def cross_level(x, z, sums, far, bit, n):
    return pl.pallas_call(
        functools.partial(cross_kernel, bit, n),
        out_shape=[
            jax.ShapeDtypeStruct(x.shape, x.dtype),
            jax.ShapeDtypeStruct(z.shape, z.dtype),
        ],
        in_specs=[VMEM] * 4,
        out_specs=[VMEM] * 2,
        compiler_params=pltpu.CompilerParams(vmem_limit_bytes=32 << 20),
        name="cross_level",
    )(x, z, sums, far)


def last_kernel(bit, n, count, slot_ref, x_ref, z_ref, sums_ref, far_ref, *outs):
    x = far_level(bit, n, x_ref, z_ref, sums_ref, far_ref)
    stretch = x.shape[0] // SLOTS
    per_head = HD // HALF
    heads = stretch // per_head
    lower = one_hot(iota((heads, stretch), 1) // per_head == iota((heads, stretch), 0))
    place = iota((stretch, LANES), 1) // HALF == iota((stretch, LANES), 0) % per_head
    home = holder()
    flat = []
    for s in range(SLOTS):
        tall = jnp.where(place, x[s * stretch:(s + 1) * stretch], 0.0).astype(jnp.bfloat16)
        flat.append(jnp.dot(lower, tall, preferred_element_type=jnp.float32))
    for k in range(count):
        second = slot_ref[1:2] == (home ^ k)
        outs[k][...] = jnp.where(second, flat[1], flat[0]).astype(jnp.bfloat16)


def last_level(slots, x, z, sums, far, bit, n, count):
    stretch = x.shape[0] // SLOTS
    heads = stretch * HALF // HD
    return pl.pallas_call(
        functools.partial(last_kernel, bit, n, count),
        out_shape=[jax.ShapeDtypeStruct((heads, HD), jnp.bfloat16)] * count,
        in_specs=[VMEM] * 5,
        out_specs=[VMEM] * count,
        compiler_params=pltpu.CompilerParams(vmem_limit_bytes=32 << 20),
        name="last_level",
    )(slots, x, z, sums, far)


def pick_kernel(count, slot_ref, *refs):
    parts, out = refs[:count], refs[count]
    which = slot_ref[SLOTS:SLOTS + 1]
    row = parts[0][...].astype(jnp.float32)
    for k in range(1, count):
        row = jnp.where(which == k, parts[k][...].astype(jnp.float32), row)
    row = row.astype(jnp.bfloat16)
    for h in range(row.shape[0]):
        out[0:1, h * HD:(h + 1) * HD] = row[h:h + 1]


def picked(slots, parts):
    heads = parts[0].shape[0]
    count = len(parts)
    return pl.pallas_call(
        functools.partial(pick_kernel, count),
        out_shape=jax.ShapeDtypeStruct((1, heads * HD), jnp.bfloat16),
        in_specs=[VMEM] * (count + 1),
        out_specs=VMEM,
        compiler_params=pltpu.CompilerParams(vmem_limit_bytes=8 << 20),
        name="pick",
    )(slots, *parts)


def shards(queries, key_cache, value_cache, lengths, languages, adapter):
    tensor, near, pipe = (lax.axis_size(a) for a in ("tensor", "dp", "pipe"))
    rows = queries.shape[0]
    holders = near * pipe
    levels, lang_share, stretch, _ = adapter.shape
    local = stretch.bit_length() - 1
    caches = [pltpu.with_memory_space_constraint(c, pltpu.HBM) for c in (key_cache, value_cache)]
    swap = [(0, 1), (1, 0)]
    sent = send_halves(*caches)
    other = [lax.ppermute(half, "pipe", swap) for half in sent]
    langs = exchange([languages] * near, "dp", near)
    spread = cores_exchange([queries] * (tensor // 2), tensor)
    wide, scores, sums = attend_own(spread, key_cache)
    *parts, slots = attend(
        langs, lengths, wide, scores, value_cache, *other, tensor // 2, lang_share
    )
    first = fetch(slots, parts[0], adapter, 0, FIRST)
    part = merged(cores_exchange(parts, tensor), first)
    second = fetch(slots, part, adapter, FIRST, local - FIRST)
    parts = exchange([part] * holders, ("dp", "pipe"), holders)
    x, z = local_levels(slots, parts, sums, (first, second), local, rows, pipe)
    far = fetch(slots, z, adapter, local, levels - local)
    for n in range(levels - local):
        z = lax.ppermute(z, "tensor", [(i, i ^ (1 << n)) for i in range(tensor)])
        if n < levels - local - 1:
            x, z = cross_level(x, z, sums, far, n, n)
        else:
            outs = last_level(slots, x, z, sums, far, n, n, holders)
    outs = exchange(outs, ("dp", "pipe"), holders)
    return picked(slots, outs)


def solution(mesh):
    in_specs = (
        P(("parts", "dp"), "tensor"),
        P(("parts", "dp"), None, ("tensor", "pipe"), None),
        P(("parts", "dp"), None, ("tensor", "pipe"), None),
        P(("parts", "dp")),
        P(("parts", "dp")),
        P(None, ("dp", "pipe"), "tensor", None),
    )
    out_specs = P(("parts", "dp", "pipe"), "tensor")
    return jax.shard_map(shards, mesh=mesh, in_specs=in_specs, out_specs=out_specs, check_vma=False)
```

```python
import functools
import math

import jax
import jax.numpy as jnp
from jax import lax
from jax.experimental import pallas as pl
from jax.experimental.pallas import tpu as pltpu
from jax.sharding import PartitionSpec as P

HQ = 128
KVH = 8
HD = 128
B = 64
HALF = B // 2
LANES = 128
SLOTS = 2
GROUP = HQ // KVH
WIDE = HALF * B
NEG = -1e30
FLOOR = -1e29
FIRST = 2
STATS = 16

VMEM = pl.BlockSpec(memory_space=pltpu.VMEM)
SMEM = pl.BlockSpec(memory_space=pltpu.SMEM)
HBM = pl.BlockSpec(memory_space=pltpu.HBM)
ANY = pl.BlockSpec(memory_space=pl.ANY)


def exchange(blocks, axis, count):
    out = [blocks[0]]
    for k in range(1, count):
        route = [(i, i ^ k) for i in range(count)]
        out.append(lax.ppermute(blocks[k], axis, route))
    return out


def by_parity(tensor):
    return HQ // tensor >= GROUP


def half_of(index, tensor):
    if by_parity(tensor):
        half = index
        for n in range(1, (tensor - 1).bit_length()):
            half = half ^ (index >> n)
        return half & 1
    return index // (tensor // 2)


def reach_of(i, p, tensor):
    if by_parity(tensor):
        return (i << 1) | (half_of(i, tensor) ^ p)
    return p * (tensor // 2) + i


def place_of(shard, tensor):
    return shard >> 1 if by_parity(tensor) else shard % (tensor // 2)


def cores_exchange(blocks, tensor):
    out = []
    for i, block in enumerate(blocks):
        route = [(2 * t + p, 2 * (t ^ reach_of(i, p, tensor)) + p) for t in range(tensor) for p in range(2)]
        out.append(lax.ppermute(block, ("tensor", "pipe"), route))
    return out


def iota(shape, dim):
    return lax.broadcasted_iota(jnp.int32, shape, dim)


def start_half(flip, src_hbm, dst_ref, sems):
    rows = dst_ref.shape[0]
    tensor = lax.axis_size("tensor")
    half = half_of(lax.axis_index("tensor"), tensor) ^ lax.axis_index("pipe") ^ flip
    size = HQ // tensor // GROUP if by_parity(tensor) else KVH // 2
    copies = []
    for r in range(rows):
        for j in range(KVH // 2 // size):
            src = pl.ds(reach_of(j, half, tensor) * size if by_parity(tensor) else half * size, size)
            copy = pltpu.make_async_copy(src_hbm.at[r, src], dst_ref.at[r, pl.ds(j * size, size)], sems.at[r, j])
            copy.start()
            copies.append(copy)
    return copies


def send_kernel(*refs):
    caches, outs, sems = refs[:2], refs[2:4], refs[4]
    copies = []
    for n in range(2):
        copies += start_half(1, caches[n], outs[n], sems.at[n])
    for copy in copies:
        copy.wait()


def send_halves(key_cache, value_cache):
    rows, _, span, _ = key_cache.shape
    half = jax.ShapeDtypeStruct((rows, KVH // 2, span, HD), key_cache.dtype)
    return pl.pallas_call(
        send_kernel,
        out_shape=[half, half],
        in_specs=[HBM, HBM],
        out_specs=[VMEM, VMEM],
        scratch_shapes=[pltpu.SemaphoreType.DMA((2, rows, KVH // 2))],
        compiler_params=pltpu.CompilerParams(vmem_limit_bytes=8 << 20),
        name="send_halves",
    )(key_cache, value_cache)


def slots_of(named, share):
    home = holder()
    d = lax.axis_index("dp")
    found = jnp.int32(0)
    row_ids = [jnp.int32(-1)] * SLOTS
    langs = [jnp.int32(0)] * SLOTS
    for k, row_langs in enumerate(named):
        rows = len(row_langs)
        for i, lang in enumerate(row_langs):
            mine = lang // share == home
            for s in range(SLOTS):
                take = mine & (found == s)
                row_ids[s] = jnp.where(take, (d ^ k) * rows + i, row_ids[s])
                langs[s] = jnp.where(take, lang - home * share, langs[s])
            found = found + mine.astype(jnp.int32)
    return row_ids, langs


def holder():
    return lax.axis_index(("dp", "pipe"))


def start_tables(first, langs, table_hbm, table_ref, sems):
    copies = []
    for k in range(table_ref.shape[0]):
        for s in range(SLOTS):
            copy = pltpu.make_async_copy(table_hbm.at[first + k, langs[s]], table_ref.at[k, s], sems.at[k, s])
            copy.start()
            copies.append(copy)
    return copies


def own_kernel(count, *refs):
    q_refs, key_ref = refs[:count], refs[count]
    wide_ref, score_ref, sums_ref = refs[count + 1:]
    rows = q_refs[0].shape[0]
    chunks, tall, _ = wide_ref.shape
    size = tall // rows
    sums_ref[...] = one_hot(iota(sums_ref.shape, 0) // B == iota(sums_ref.shape, 1) % HALF)
    which = iota((tall, HD), 0) % rows
    for n in range(chunks):
        k, c = divmod(n, chunks // count)
        q = jnp.concatenate(
            [q_refs[k][:, h * HD:(h + 1) * HD] for h in range(c * size, (c + 1) * size)], axis=0
        )
        q = jnp.concatenate([jnp.where(which == r, q, jnp.zeros_like(q)) for r in range(rows)], axis=1)
        wide_ref[n] = q
        score_ref[n] = scores_of(q, key_ref, group_of(n, chunks, count, size, True))


def beside(ref, group):
    return jnp.concatenate([ref[r, group] for r in range(ref.shape[0])], axis=1)


def scores_of(wide, key_ref, group):
    return lax.dot_general(
        wide, beside(key_ref, group), (((1,), (1,)), ((), ())), preferred_element_type=jnp.float32
    )


def group_of(n, chunks, count, size, of_all=False):
    k, c = divmod(n, chunks // count)
    tensor = 2 * count
    shard = lax.axis_index("tensor") ^ reach_of(k, lax.axis_index("pipe"), tensor)
    place = shard if of_all else place_of(shard, tensor)
    return (place * (HQ // tensor) + c * size) // GROUP


def attend_own(queries, key_cache):
    count = len(queries)
    rows, width = queries[0].shape
    share = width // HD
    size = min(GROUP, share)
    span = key_cache.shape[2]
    chunks, tall = count * share // size, size * rows
    return pl.pallas_call(
        functools.partial(own_kernel, count),
        out_shape=[
            jax.ShapeDtypeStruct((chunks, tall, rows * HD), jnp.bfloat16),
            jax.ShapeDtypeStruct((chunks, tall, span), jnp.float32),
            jax.ShapeDtypeStruct((WIDE, LANES), jnp.bfloat16),
        ],
        in_specs=[VMEM] * (count + 1),
        out_specs=[VMEM] * 3,
        compiler_params=pltpu.CompilerParams(vmem_limit_bytes=16 << 20),
        name="attend_own",
    )(*queries, key_cache)


def attend_kernel(count, near, length_any, *refs):
    refs = refs[near:]
    wide_ref, score_ref, own_value_ref, key_ref, value_ref = refs[:5]
    out_refs, (length_ref, length_sem) = refs[5:count + 5], refs[count + 5:]
    length_copy = pltpu.make_async_copy(length_any, length_ref, length_sem)
    length_copy.start()
    rows, _, span, _ = key_ref.shape
    chunks, tall, _ = wide_ref.shape
    size = tall // rows
    share = size * (chunks // count)
    t, p = lax.axis_index("tensor"), lax.axis_index("pipe")
    other = [
        scores_of(wide_ref[n], key_ref, group_of(n, chunks, count, size)) for n in range(chunks)
    ]
    length_copy.wait()
    block = share * rows
    spot = iota((tall, LANES), 1) % block - iota((tall, LANES), 0)
    tops, totals = [0.0] * count, [0.0] * count
    place = iota((tall, 2 * span), 1)
    start = jnp.where(place < span, p, (1 ^ p) - 1) + 2 * t
    which = iota((tall, 2 * span), 0) % rows
    length = length_ref[0]
    for r in range(1, rows):
        length = jnp.where(which == r, length_ref[r], length)
    visible = start * span + place < length
    for n in range(chunks):
        k, c = divmod(n, chunks // count)
        group, whole = group_of(n, chunks, count, size), group_of(n, chunks, count, size, True)
        scores = jnp.concatenate([score_ref[n], other[n]], axis=1)
        scores = jnp.where(visible, scores * (1.0 / math.sqrt(HD)), NEG)
        top = jnp.maximum(jnp.max(scores, axis=1, keepdims=True), FLOOR)
        top = top.astype(jnp.bfloat16).astype(jnp.float32)
        weights = jnp.exp(scores - top)
        total = jnp.sum(weights, axis=1, keepdims=True)
        weights = weights.astype(jnp.bfloat16)
        both = sum(
            jnp.dot(
                weights[:, side * span:(side + 1) * span],
                beside(values, place),
                preferred_element_type=jnp.float32,
            )
            for side, (values, place) in enumerate(((own_value_ref, whole), (value_ref, group)))
        )
        which = iota((tall, LANES), 0) % rows
        weighted = both[:, :HD]
        for r in range(1, rows):
            weighted = jnp.where(which == r, both[:, r * HD:(r + 1) * HD], weighted)
        out_refs[k][c * tall:(c + 1) * tall] = weighted.astype(jnp.bfloat16)
        here = spot == c * tall
        tops[k] = tops[k] + jnp.sum(jnp.where(here, top, 0.0), axis=0, keepdims=True)
        totals[k] = totals[k] + jnp.sum(jnp.where(here, total, 0.0), axis=0, keepdims=True)
    for k in range(count):
        out_refs[k][block:] = stats(tops[k], totals[k])


def stats(top, total):
    coarse = total.astype(jnp.bfloat16).astype(jnp.float32)
    row = iota((STATS, LANES), 0)
    out = jnp.where(row == 0, top, jnp.where(row == 1, coarse, jnp.where(row == 2, total - coarse, 0.0)))
    return out.astype(jnp.bfloat16)


def factors(parts):
    tops, totals = [], []
    for part in parts:
        rows = part[part.shape[0] - STATS:].astype(jnp.float32)
        tops.append(rows[0:1])
        totals.append(rows[1:2] + rows[2:3])
    peak = functools.reduce(jnp.maximum, tops)
    scale = [jnp.exp(top - peak) for top in tops]
    return scale, peak, sum(f * total for f, total in zip(scale, totals))


def weigh(scale, mask, block):
    coarse = scale.astype(jnp.bfloat16).astype(jnp.float32)
    side = iota((1, LANES), 1) // block
    both = jnp.where(side == 0, coarse, jnp.where(side == 1, scale - coarse, 0.0))
    return jnp.where(mask, both, 0.0).astype(jnp.bfloat16)


def stacked(parts, block):
    return jnp.concatenate([part[:block] for part in parts for _ in range(LANES // block)], axis=0)


def attend(lengths, langs, wide, scores, own_value, key, value, count):
    near = len(langs)
    chunks, tall, _ = wide.shape
    rows = key.shape[0]
    chunk = jax.ShapeDtypeStruct((chunks // count * tall + STATS, LANES), jnp.bfloat16)
    return pl.pallas_call(
        functools.partial(attend_kernel, count, near),
        out_shape=[chunk] * count,
        in_specs=[ANY] * (near + 1) + [VMEM] * 5,
        out_specs=[VMEM] * count,
        scratch_shapes=[pltpu.SMEM((rows,), jnp.int32), pltpu.SemaphoreType.DMA],
        compiler_params=pltpu.CompilerParams(vmem_limit_bytes=16 << 20),
        name="attend",
    )(lengths, *langs, wide, scores, own_value, key, value)


def first_kernel(near, *refs):
    lang_refs, (_, table_hbm, table_ref, slot_ref, sems) = refs[:near], refs[near:]
    share = table_hbm.shape[1]
    named = []
    for lang_ref in lang_refs:
        vector = lang_ref[...].astype(jnp.float32)
        lane = iota(vector.shape, 1)
        named.append(
            [
                jnp.max(jnp.where(lane == i, vector, -1.0)).astype(jnp.int32)
                for i in range(vector.shape[1])
            ]
        )
    row_ids, langs = slots_of(named, share)
    copies = start_tables(0, langs, table_hbm, table_ref, sems)
    pipe = lax.axis_index("pipe")
    own = named[0][0]
    for i in range(1, len(named[0])):
        own = jnp.where(pipe == i, named[0][i], own)
    row = iota(slot_ref.shape, 0)
    slots = jnp.where(row == SLOTS, (own // share) ^ holder(), -1)
    for s in range(SLOTS):
        slots = jnp.where(row == s, row_ids[s], slots)
        slots = jnp.where(row == SLOTS + 1 + s, langs[s], slots)
    slot_ref[...] = slots
    for copy in copies:
        copy.wait()


def fetch_first(langs, after, adapter, count):
    _, _, stretch, wide = adapter.shape
    near = len(langs)
    return pl.pallas_call(
        functools.partial(first_kernel, near),
        out_shape=[
            jax.ShapeDtypeStruct((count, SLOTS, stretch, wide), jnp.bfloat16),
            jax.ShapeDtypeStruct((8, LANES), jnp.int32),
        ],
        in_specs=[VMEM] * near + [ANY, HBM],
        out_specs=[VMEM, VMEM],
        scratch_shapes=[pltpu.SemaphoreType.DMA((count, SLOTS))],
        compiler_params=pltpu.CompilerParams(vmem_limit_bytes=16 << 20),
        name="fetch_first",
    )(*langs, after, adapter)


def fetch_kernel(first, slot_ref, _, table_hbm, table_ref, sems):
    places = slot_ref[SLOTS + 1:2 * SLOTS + 1].astype(jnp.float32)
    langs = [jnp.max(places[s:s + 1]).astype(jnp.int32) for s in range(SLOTS)]
    for copy in start_tables(first, langs, table_hbm, table_ref, sems):
        copy.wait()


def fetch(slots, after, adapter, first, count):
    _, _, stretch, wide = adapter.shape
    return pl.pallas_call(
        functools.partial(fetch_kernel, first),
        out_shape=jax.ShapeDtypeStruct((count, SLOTS, stretch, wide), jnp.bfloat16),
        in_specs=[VMEM, ANY, HBM],
        out_specs=VMEM,
        scratch_shapes=[pltpu.SemaphoreType.DMA((count, SLOTS))],
        compiler_params=pltpu.CompilerParams(vmem_limit_bytes=16 << 20),
        name="fetch",
    )(slots, after, adapter)


def merge_kernel(count, *refs):
    out = refs[-1]
    parts = [refs[k][...] for k in range(count)]
    block = out.shape[0] - STATS
    scale, peak, total = factors(parts)
    mask = iota((block, LANES), 1) % block == iota((block, LANES), 0)
    matrix = jnp.concatenate([weigh(f, mask, block) for f in scale], axis=1)
    weighted = jnp.dot(matrix, stacked(parts, block), preferred_element_type=jnp.float32)
    out[:block] = weighted.astype(jnp.bfloat16)
    out[block:] = stats(peak, total)


def merged(parts, after):
    return pl.pallas_call(
        functools.partial(merge_kernel, len(parts)),
        out_shape=jax.ShapeDtypeStruct(parts[0].shape, parts[0].dtype),
        in_specs=[VMEM] * len(parts) + [ANY],
        out_specs=VMEM,
        compiler_params=pltpu.CompilerParams(vmem_limit_bytes=8 << 20),
        name="merge",
    )(*parts, after)


def one_hot(cond):
    return jnp.where(cond, 1.0, 0.0).astype(jnp.bfloat16)


def level(own, partner, upper, table, sums):
    lane_upper = iota(own.shape, 1) // HALF % 2
    paired = jnp.where(lane_upper == upper, own, partner).astype(jnp.bfloat16)
    products = jnp.concatenate(
        [table[:, c * LANES:(c + 1) * LANES] * paired for c in range(WIDE // LANES)], axis=1
    )
    y = jnp.dot(products, sums, preferred_element_type=jnp.float32)
    return y.astype(jnp.bfloat16).astype(jnp.float32)


def packed(x):
    quarter = x.shape[0] // 4
    block = iota((quarter, LANES), 1) // HALF
    out = x[0:quarter]
    for n in range(1, 4):
        out = jnp.where(block == n, x[n * quarter:(n + 1) * quarter], out)
    return out.astype(jnp.bfloat16)


def unpacked(z):
    row, col = iota((LANES, LANES), 0), iota((LANES, LANES), 1)
    return jnp.concatenate(
        [
            jnp.dot(z, one_hot(row == n * HALF + col % HALF), preferred_element_type=jnp.float32)
            for n in range(4)
        ],
        axis=0,
    )


def local_kernel(count, groups, local, rows, pipe_count, slot_ref, sums_ref, *refs):
    tables, parts, (x_ref, z_ref) = refs[:groups], refs[groups:groups + count], refs[groups + count:]
    stretch = tables[0].shape[2]
    near = count // pipe_count
    block = parts[0].shape[0] - STATS
    per_head = HD // HALF
    d = lax.axis_index("dp")
    parts = [part[...] for part in parts]
    shape = (stretch, LANES)
    lane = iota(shape, 1) % block
    same_head = iota(shape, 0) // per_head == lane // rows
    place = iota(shape, 1) // HALF == iota(shape, 0) % per_head
    spread = one_hot(iota((LANES, LANES), 0) % HALF == iota((LANES, LANES), 1) % HALF)
    columns = [[] for _ in range(SLOTS)]
    for k in range(near):
        pair = parts[k * pipe_count:(k + 1) * pipe_count]
        scale, _, total = factors(pair)
        row = (d ^ k) * rows + lane % rows
        for s in range(SLOTS):
            mask = same_head & (row == slot_ref[s:s + 1])
            columns[s] += [weigh(f / total, mask, block) for f in scale]
    matrix = jnp.concatenate([jnp.concatenate(c, axis=1) for c in columns], axis=0)
    tall = jnp.dot(matrix, stacked(parts, block), preferred_element_type=jnp.float32)
    place = jnp.concatenate([place] * SLOTS, axis=0)
    tall = jnp.where(place, tall, 0.0).astype(jnp.bfloat16)
    xs = [
        jnp.dot(tall[s * stretch:(s + 1) * stretch], spread, preferred_element_type=jnp.float32)
        for s in range(SLOTS)
    ]
    index = iota(shape, 0)
    sums = sums_ref[...]
    for k in range(local):
        reach = 1 << k
        upper = index // reach % 2
        table, at = table_of(tables, k)
        for s in range(SLOTS):
            ahead = jnp.roll(xs[s], -reach, axis=0)
            behind = jnp.roll(xs[s], reach, axis=0)
            partner = jnp.where(upper == 0, ahead, behind)
            xs[s] = level(xs[s], partner, upper, table.at[at, s], sums)
    x = jnp.concatenate(xs, axis=0)
    x_ref[...] = x.astype(jnp.bfloat16)
    z_ref[...] = packed(x)


def table_of(tables, k):
    for table in tables:
        if k < table.shape[0]:
            return table, k
        k -= table.shape[0]


def local_levels(slots, parts, sums, tables, local, rows, pipe_count):
    stretch = tables[0].shape[2]
    count = len(parts)
    shape = (SLOTS * stretch, LANES)
    return pl.pallas_call(
        functools.partial(local_kernel, count, len(tables), local, rows, pipe_count),
        out_shape=[
            jax.ShapeDtypeStruct(shape, jnp.bfloat16),
            jax.ShapeDtypeStruct((shape[0] // 4, LANES), jnp.bfloat16),
        ],
        in_specs=[VMEM] * (count + len(tables) + 2),
        out_specs=[VMEM] * 2,
        compiler_params=pltpu.CompilerParams(vmem_limit_bytes=24 << 20),
        name="local_levels",
    )(slots, sums, *tables, *parts)


def far_level(bit, n, x_ref, z_ref, sums_ref, far_ref):
    upper = lax.axis_index("tensor") // (1 << bit) % 2
    partner = unpacked(z_ref[...])
    stretch = x_ref.shape[0] // SLOTS
    sums = sums_ref[...]
    out = []
    for s in range(SLOTS):
        part = slice(s * stretch, (s + 1) * stretch)
        out.append(level(x_ref[part].astype(jnp.float32), partner[part], upper, far_ref.at[n, s], sums))
    return jnp.concatenate(out, axis=0)


def cross_kernel(bit, n, x_ref, z_ref, sums_ref, far_ref, x_out, z_out):
    x = far_level(bit, n, x_ref, z_ref, sums_ref, far_ref)
    x_out[...] = x.astype(jnp.bfloat16)
    z_out[...] = packed(x)


def cross_level(x, z, sums, far, bit, n):
    return pl.pallas_call(
        functools.partial(cross_kernel, bit, n),
        out_shape=[
            jax.ShapeDtypeStruct(x.shape, x.dtype),
            jax.ShapeDtypeStruct(z.shape, z.dtype),
        ],
        in_specs=[VMEM] * 4,
        out_specs=[VMEM] * 2,
        compiler_params=pltpu.CompilerParams(vmem_limit_bytes=32 << 20),
        name="cross_level",
    )(x, z, sums, far)


def last_kernel(bit, n, count, slot_ref, x_ref, z_ref, sums_ref, far_ref, *outs):
    x = far_level(bit, n, x_ref, z_ref, sums_ref, far_ref)
    stretch = x.shape[0] // SLOTS
    per_head = HD // HALF
    heads = stretch // per_head
    lower = one_hot(iota((heads, stretch), 1) // per_head == iota((heads, stretch), 0))
    place = iota((stretch, LANES), 1) // HALF == iota((stretch, LANES), 0) % per_head
    home = holder()
    flat = []
    for s in range(SLOTS):
        tall = jnp.where(place, x[s * stretch:(s + 1) * stretch], 0.0).astype(jnp.bfloat16)
        flat.append(jnp.dot(lower, tall, preferred_element_type=jnp.float32))
    for k in range(count):
        second = slot_ref[1:2] == (home ^ k)
        outs[k][...] = jnp.where(second, flat[1], flat[0]).astype(jnp.bfloat16)


def last_level(slots, x, z, sums, far, bit, n, count):
    stretch = x.shape[0] // SLOTS
    heads = stretch * HALF // HD
    return pl.pallas_call(
        functools.partial(last_kernel, bit, n, count),
        out_shape=[jax.ShapeDtypeStruct((heads, HD), jnp.bfloat16)] * count,
        in_specs=[VMEM] * 5,
        out_specs=[VMEM] * count,
        compiler_params=pltpu.CompilerParams(vmem_limit_bytes=32 << 20),
        name="last_level",
    )(slots, x, z, sums, far)


def pick_kernel(count, slot_ref, *refs):
    parts, out = refs[:count], refs[count]
    which = slot_ref[SLOTS:SLOTS + 1]
    row = parts[0][...].astype(jnp.float32)
    for k in range(1, count):
        row = jnp.where(which == k, parts[k][...].astype(jnp.float32), row)
    row = row.astype(jnp.bfloat16)
    for h in range(row.shape[0]):
        out[0:1, h * HD:(h + 1) * HD] = row[h:h + 1]


def picked(slots, parts):
    heads = parts[0].shape[0]
    count = len(parts)
    return pl.pallas_call(
        functools.partial(pick_kernel, count),
        out_shape=jax.ShapeDtypeStruct((1, heads * HD), jnp.bfloat16),
        in_specs=[VMEM] * (count + 1),
        out_specs=VMEM,
        compiler_params=pltpu.CompilerParams(vmem_limit_bytes=8 << 20),
        name="pick",
    )(slots, *parts)


def shards(queries, key_cache, value_cache, lengths, languages, adapter):
    tensor, near, pipe = (lax.axis_size(a) for a in ("tensor", "dp", "pipe"))
    rows = queries.shape[0]
    holders = near * pipe
    levels, _, stretch, _ = adapter.shape
    local = stretch.bit_length() - 1
    caches = [pltpu.with_memory_space_constraint(c, pltpu.HBM) for c in (key_cache, value_cache)]
    swap = [(0, 1), (1, 0)]
    sent = send_halves(*caches)
    other = [lax.ppermute(half, "pipe", swap) for half in sent]
    langs = exchange([languages.reshape(1, rows)] * near, "dp", near)
    spread = cores_exchange([queries] * (tensor // 2), tensor)
    wide, scores, sums = attend_own(spread, key_cache)
    parts = attend(lengths, langs, wide, scores, value_cache, *other, tensor // 2)
    first, slots = fetch_first(langs, parts[0], adapter, FIRST)
    part = merged(cores_exchange(parts, tensor), first)
    second = fetch(slots, part, adapter, FIRST, local - FIRST)
    parts = exchange([part] * holders, ("dp", "pipe"), holders)
    x, z = local_levels(slots, parts, sums, (first, second), local, rows, pipe)
    far = fetch(slots, z, adapter, local, levels - local)
    for n in range(levels - local):
        z = lax.ppermute(z, "tensor", [(i, i ^ (1 << n)) for i in range(tensor)])
        if n < levels - local - 1:
            x, z = cross_level(x, z, sums, far, n, n)
        else:
            outs = last_level(slots, x, z, sums, far, n, n, holders)
    outs = exchange(outs, ("dp", "pipe"), holders)
    return picked(slots, outs)


def solution(mesh):
    in_specs = (
        P(("parts", "dp"), "tensor"),
        P(("parts", "dp"), None, ("tensor", "pipe"), None),
        P(("parts", "dp"), None, ("tensor", "pipe"), None),
        P(("parts", "dp")),
        P(("parts", "dp")),
        P(None, ("dp", "pipe"), "tensor", None),
    )
    out_specs = P(("parts", "dp", "pipe"), "tensor")
    return jax.shard_map(shards, mesh=mesh, in_specs=in_specs, out_specs=out_specs, check_vma=False)
```
